32 devices in a mesh: dp: 16 (over z, y, core), tensor: 2 (over x).
Axes of the slice: x: 2, y: 2, z: 4, core: 2. Of those that a mesh axis runs over, the one named last changes fastest.
Arguments:
- layer_input: bfloat16 [32768, 1024], P(('dp', 'tensor')), may hold values from -6 to 6
- attention_norm: float32 [1024], replicated, may hold values from 0.25 to 1.75
- query_weight: bfloat16 [1024, 2048], P('dp', 'tensor'), may hold values from -0.1875 to 0.1875
- key_matrix: bfloat16 [1024, 1024], P('dp', 'tensor'), may hold values from -0.1875 to 0.1875
- value_matrix: bfloat16 [1024, 1024], P('dp', 'tensor'), may hold values from -0.1875 to 0.1875
- query_norm: float32 [128], replicated, may hold values from 0.25 to 1.75
- key_norm: float32 [128], replicated, may hold values from 0.25 to 1.75
- output_weight: bfloat16 [2048, 1024], P('tensor', 'dp'), may hold values from -0.5 to 0.5
- feedforward_norm: float32 [1024], replicated, may hold values from 0.25 to 1.75
- gate_weight: bfloat16 [1024, 3072], P('dp', 'tensor'), may hold values from -0.1875 to 0.1875
- up_weight: bfloat16 [1024, 3072], P('dp', 'tensor'), may hold values from -0.1875 to 0.1875
- down_weight: bfloat16 [3072, 1024], P('tensor', 'dp'), may hold values from -0.109375 to 0.109375
- out_grad: bfloat16 [32768, 1024], P(('dp', 'tensor')), may hold values from -6 to 6
Outputs:
- layer_output: bfloat16 [32768, 1024], P(('dp', 'tensor'))
- input_grad: float32 [32768, 1024], P(('dp', 'tensor'))
- attention_norm_grad: float32 [1024], replicated
- query_weight_grad: float32 [1024, 2048], P('dp', 'tensor')
- key_weight_grad: float32 [1024, 1024], P('dp', 'tensor')
- value_weight_grad: float32 [1024, 1024], P('dp', 'tensor')
- query_norm_grad: float32 [128], replicated
- key_norm_grad: float32 [128], replicated
- output_weight_grad: float32 [2048, 1024], P('tensor', 'dp')
- feedforward_norm_grad: float32 [1024], replicated
- gate_weight_grad: float32 [1024, 3072], P('dp', 'tensor')
- up_weight_grad: float32 [1024, 3072], P('dp', 'tensor')
- down_weight_grad: float32 [3072, 1024], P('tensor', 'dp')
The draws below stay inside these ranges and needn't reach their ends.
All inputs are finite; a program needn't handle non-finite values.
Results may differ from the reference program's by a relative error of at most 0.019.
Values may be sent and summed in bfloat16 or wider, within the bound.
No kernel may reach another device: no remote copies, remote signals or barrier semaphores. Data moves between devices by JAX's collectives and lax.ppermute only.
A program may use at most 320 MiB of HBM per device.

```python
import jax
import jax.numpy as jnp
from jax import lax

MODEL_WIDTH = 1024
QUERY_HEAD_COUNT = 16
KEY_VALUE_HEADS = 8
HEAD_SIZE = 128
FF = 3072
SEQ_LEN = 2048
SEQS = 16
TOKENS = 32768


def spiked(array, rng, source, target, shards_of, factor):
    def block_of(axis_at):
        return (jnp.arange(array.shape[axis_at]) // (array.shape[axis_at] // shards_of)).reshape((-1,) + (1,) * (array.ndim - 1 - axis_at))

    near = jax.random.permutation(rng, shards_of)[block_of(target)]
    second = (block_of(target) + shards_of // 2) % shards_of
    return jnp.where((block_of(source) == near) | (block_of(source) == second), factor * array, array)


def block_levels(rng, extent, split, smallest, largest):
    loudness = 1.0
    for dim, shards_of in split:
        heights = jax.random.uniform(jax.random.fold_in(jax.random.fold_in(rng, 6), dim), (shards_of,), jnp.float32, smallest / len(split), largest / len(split))
        loudness = loudness * jnp.repeat(jnp.exp(heights), extent[dim] // shards_of).reshape((-1,) + (1,) * (len(extent) - 1 - dim))
    return loudness


def gaussian(stream_key, extent, deviation, reach, pieces=(), dtype=jnp.bfloat16):
    entries = deviation * jax.random.normal(stream_key, extent, jnp.float32)
    if pieces:
        entries = entries * block_levels(stream_key, extent, pieces, -0.22, 0.18)
    return jnp.clip(entries, -reach, reach).astype(dtype)


def heavy_noise(own_key, extent, deviation, reach, shards, heavy, dtype=jnp.bfloat16):
    drawn = deviation * jax.random.normal(own_key, extent, jnp.float32)
    if shards:
        drawn = drawn * block_levels(own_key, extent, shards, -0.22, 0.18)
    return jnp.clip(spiked(drawn, jax.random.fold_in(own_key, 3), *heavy), -reach, reach).astype(dtype)


def setup_inputs(seed: int = 0) -> dict:
    splits = jax.random.split(jax.random.key(seed), 14)
    layer_input = gaussian(splits[0], (TOKENS, MODEL_WIDTH), 1.0, 6.0, ((0, 32),))
    attention_norm = jnp.clip(1.0 + 0.15 * jax.random.normal(splits[1], (MODEL_WIDTH,), jnp.float32), 0.25, 1.75)
    query_weight = gaussian(splits[2], (MODEL_WIDTH, QUERY_HEAD_COUNT * HEAD_SIZE), MODEL_WIDTH ** -0.5, 0.1875, ((0, 16), (1, 2)))
    key_matrix = gaussian(splits[3], (MODEL_WIDTH, KEY_VALUE_HEADS * HEAD_SIZE), MODEL_WIDTH ** -0.5, 0.1875, ((0, 16), (1, 2)))
    value_matrix = gaussian(splits[4], (MODEL_WIDTH, KEY_VALUE_HEADS * HEAD_SIZE), MODEL_WIDTH ** -0.5, 0.1875, ((0, 16), (1, 2)))
    query_norm = jnp.clip(1.0 + 0.15 * jax.random.normal(splits[5], (HEAD_SIZE,), jnp.float32), 0.25, 1.75)
    key_norm = jnp.clip(1.0 + 0.15 * jax.random.normal(splits[6], (HEAD_SIZE,), jnp.float32), 0.25, 1.75)
    output_weight = gaussian(splits[7], (QUERY_HEAD_COUNT * HEAD_SIZE, MODEL_WIDTH), (QUERY_HEAD_COUNT * HEAD_SIZE // 16) ** -0.5, 0.5, ((0, 2), (1, 16)))
    feedforward_norm = jnp.clip(1.0 + 0.15 * jax.random.normal(splits[8], (MODEL_WIDTH,), jnp.float32), 0.25, 1.75)
    gate_weight = gaussian(splits[9], (MODEL_WIDTH, FF), MODEL_WIDTH ** -0.5, 0.1875, ((0, 16), (1, 2)))
    up_weight = gaussian(splits[10], (MODEL_WIDTH, FF), MODEL_WIDTH ** -0.5, 0.1875, ((0, 16), (1, 2)))
    down_weight = gaussian(splits[11], (FF, MODEL_WIDTH), FF ** -0.5, 0.109375, ((0, 2), (1, 16)))
    out_grad = heavy_noise(splits[12], (TOKENS, MODEL_WIDTH), 1.0, 6.0, ((0, 32),), (0, 1, 32, 2.75))
    return {"layer_input": layer_input, "attention_norm": attention_norm, "query_weight": query_weight, "key_matrix": key_matrix, "value_matrix": value_matrix, "query_norm": query_norm, "key_norm": key_norm, "output_weight": output_weight, "feedforward_norm": feedforward_norm, "gate_weight": gate_weight, "up_weight": up_weight, "down_weight": down_weight, "out_grad": out_grad}


@jax.custom_vjp
def lowered_precision(v):
    return lax.optimization_barrier(v.astype(jnp.bfloat16)).astype(jnp.float32)

@jax.custom_vjp
def lowered_backward(v):
    return v

def low_keep(v):
    return (lowered_precision(v), None)

def low_pass(kept, grad):
    return (grad,)

def back_keep(v):
    return (v, None)

def back_low(kept, grad):
    return (lowered_precision(grad),)
lowered_precision.defvjp(low_keep, low_pass)
lowered_backward.defvjp(back_keep, back_low)
epsilon = 1e-06
rope_base = 1000000.0
masked_score = -1e+30

def matrix_product(left, right):
    return jnp.dot(left, right, precision=lax.Precision.HIGHEST, preferred_element_type=jnp.float32)

def rms_norm(values, gain):
    return values * lax.rsqrt(lax.optimization_barrier(jnp.mean(values * values, axis=-1, keepdims=True)) + epsilon) * gain

def rope_tables(sequence_length):
    position = jnp.arange(sequence_length).astype(jnp.float32)
    inverse = jnp.power(rope_base, -jnp.arange(HEAD_SIZE // 2).astype(jnp.float32) * (2.0 / HEAD_SIZE))
    angles = position[:, None] * inverse[None, :]
    return (jnp.cos(angles), jnp.sin(angles))

def rotary(values, cosine, sine):
    half = values.shape[-1] // 2
    first = values[..., :half]
    second = values[..., half:]
    cos_wide = cosine[:, None, :]
    sin_wide = sine[:, None, :]
    return jnp.concatenate([first * cos_wide - second * sin_wide, second * cos_wide + first * sin_wide], axis=-1)

def attend_block(query_block, start, keys, values_in):
    block_slice = query_block.shape[0]
    raw = jnp.einsum('qcgd,kcd->cgqk', query_block, keys, precision=lax.Precision.HIGHEST, preferred_element_type=jnp.float32)
    scores = lowered_backward(raw * HEAD_SIZE ** (-0.5))
    rows = start + jnp.arange(block_slice).astype(jnp.int32)
    columns = jnp.arange(keys.shape[0]).astype(jnp.int32)
    allowed = columns[None, :] <= rows[:, None]
    scores = jnp.where(allowed, scores, masked_score)
    top = lax.optimization_barrier(jnp.max(scores, axis=-1, keepdims=True))
    exps = jnp.exp(scores - top)
    probs = exps / lax.optimization_barrier(jnp.sum(exps, axis=-1, keepdims=True))
    mixed = jnp.einsum('cgqk,kcd->qcgd', lowered_precision(probs), values_in, precision=lax.Precision.HIGHEST, preferred_element_type=jnp.float32)
    return lowered_precision(lowered_backward(mixed))

def layer_sequence(sequence, params):
    norm_one, query_weight, key_matrix, value_matrix, query_norm, key_norm, output_weight, norm_two, gate_weight, up_weight, down_weight = params
    sequence_length = sequence.shape[0]
    head_ratio = QUERY_HEAD_COUNT // KEY_VALUE_HEADS
    attention_layer_input = lowered_precision(rms_norm(sequence, norm_one))
    query_raw = lowered_backward(matrix_product(attention_layer_input, query_weight)).reshape(sequence_length, QUERY_HEAD_COUNT, HEAD_SIZE)
    key_unrotated = lowered_backward(matrix_product(attention_layer_input, key_matrix)).reshape(sequence_length, KEY_VALUE_HEADS, HEAD_SIZE)
    value_lowered = lowered_precision(lowered_backward(matrix_product(attention_layer_input, value_matrix))).reshape(sequence_length, KEY_VALUE_HEADS, HEAD_SIZE)
    cosine, sine = rope_tables(sequence_length)
    query_rotated = lowered_precision(rotary(rms_norm(query_raw, query_norm), cosine, sine))
    key_rot = lowered_precision(rotary(rms_norm(key_unrotated, key_norm), cosine, sine))
    block_slice = min(512, sequence_length)
    item_count = sequence_length // block_slice
    block_list = query_rotated.reshape(item_count, block_slice, KEY_VALUE_HEADS, head_ratio, HEAD_SIZE)
    starts = jnp.arange(item_count).astype(jnp.int32) * block_slice
    mixed = lax.map(jax.checkpoint(lambda item: attend_block(item[0], item[1], key_rot, value_lowered)), (block_list, starts))
    mixed = mixed.reshape(sequence_length, QUERY_HEAD_COUNT * HEAD_SIZE)
    residual = sequence + lowered_backward(matrix_product(mixed, output_weight))
    ffn_input = lowered_precision(rms_norm(residual, norm_two))
    gate = lowered_backward(matrix_product(ffn_input, gate_weight))
    up_part = lowered_backward(matrix_product(ffn_input, up_weight))
    hidden = lowered_precision(jax.nn.silu(gate) * up_part)
    return residual + lowered_backward(matrix_product(hidden, down_weight))

def reference(layer_input, attention_norm, query_weight, key_matrix, value_matrix, query_norm, key_norm, output_weight, feedforward_norm, gate_weight, up_weight, down_weight, out_grad):
    params = (attention_norm.astype(jnp.float32), query_weight.astype(jnp.float32), key_matrix.astype(jnp.float32), value_matrix.astype(jnp.float32), query_norm.astype(jnp.float32), key_norm.astype(jnp.float32), output_weight.astype(jnp.float32), feedforward_norm.astype(jnp.float32), gate_weight.astype(jnp.float32), up_weight.astype(jnp.float32), down_weight.astype(jnp.float32))
    sequences = layer_input.astype(jnp.float32).reshape(SEQS, SEQ_LEN, MODEL_WIDTH)

    def whole(seq_all, weights):
        return lax.map(jax.checkpoint(lambda one: layer_sequence(one, weights)), seq_all)
    output, pull = jax.vjp(whole, sequences, params)
    grad_in, grads = pull(out_grad.astype(jnp.float32).reshape(SEQS, SEQ_LEN, MODEL_WIDTH))
    return (output.reshape(TOKENS, MODEL_WIDTH).astype(jnp.bfloat16), grad_in.reshape(TOKENS, MODEL_WIDTH), grads[0], grads[1], grads[2], grads[3], grads[4], grads[5], grads[6], grads[7], grads[8], grads[9], grads[10])
```

```python
import math

import jax
import jax.numpy as jnp
from jax import lax
from jax.experimental import pallas as pl
from jax.experimental.pallas import tpu as pltpu
from jax.sharding import PartitionSpec as P

HEAD_SIZE = 128
SEQ_LEN = 2048

epsilon = 1e-06
rope_base = 1000000.0
masked_score = -1e30
LN2 = math.log(2.0)
SCORE_SCALE = HEAD_SIZE ** (-0.5)
GROUP = 4 * HEAD_SIZE
F32 = jnp.float32
BF16 = jnp.bfloat16
VMEM_LIMIT = 60 * 1024 * 1024
HALF = SEQ_LEN // 2


def nn(left, right):
    return lax.dot_general(left, right, (((1,), (0,)), ((), ())), preferred_element_type=F32)


def nt(left, right):
    return lax.dot_general(left, right, (((1,), (1,)), ((), ())), preferred_element_type=F32)


def rope_tables():
    position = jnp.arange(SEQ_LEN).astype(F32)
    inverse = jnp.power(rope_base, -jnp.arange(HEAD_SIZE // 2).astype(F32) * (2.0 / HEAD_SIZE))
    angles = position[:, None] * inverse[None, :]
    cosine, sine = jnp.cos(angles), jnp.sin(angles)
    return (
        jnp.concatenate([cosine, cosine], axis=1),
        jnp.concatenate([-sine, sine], axis=1),
    )


def params(*semantics):
    return pltpu.CompilerParams(dimension_semantics=semantics, vmem_limit_bytes=VMEM_LIMIT)


def whole(shape):
    return pl.BlockSpec(shape, lambda *_: (0,) * len(shape), pipeline_mode=pl.Buffered(1))


def out_weight_spec(width, heads):
    return pl.BlockSpec((width, heads), lambda *_: (0, 2), pipeline_mode=pl.Buffered(1))


def project_kernel(x_ref, gain_ref, w_ref, qn_ref, kn_ref, cos_ref, sin_ref, at_ref, raw_ref, rot_ref):
    x = x_ref[...].astype(F32)
    scale = lax.rsqrt(jnp.mean(x * x, axis=-1, keepdims=True) + epsilon)
    a = (x * scale * gain_ref[...]).astype(BF16)
    at_ref[...] = a.T
    cosine, sine = cos_ref[...], sin_ref[...]
    for group in range(w_ref.shape[1] // GROUP):
        base = group * GROUP
        y = nn(a, w_ref[:, base : base + GROUP])
        raw_ref[:, base : base + GROUP] = y.astype(BF16)
        for head in range(3):
            z = y[:, head * HEAD_SIZE : (head + 1) * HEAD_SIZE]
            gain = kn_ref[...] * (SCORE_SCALE / LN2) if head == 2 else qn_ref[...]
            z = z * lax.rsqrt(jnp.mean(z * z, axis=-1, keepdims=True) + epsilon) * gain
            z = z * cosine + pltpu.roll(z, HEAD_SIZE // 2, 1) * sine
            rot_ref[:, base + head * HEAD_SIZE : base + (head + 1) * HEAD_SIZE] = z.astype(BF16)
        rot_ref[:, base + 3 * HEAD_SIZE : base + GROUP] = y[:, 3 * HEAD_SIZE :].astype(BF16)


def project(x, gain, weights, query_norm, key_norm, cosine, sine):
    tokens, width = x.shape
    columns = weights.shape[1] // 3 * 2
    rows = 256
    return pl.pallas_call(
        project_kernel,
        grid=(tokens // rows,),
        in_specs=[
            pl.BlockSpec((rows, width), lambda i: (i, 0)),
            whole((1, width)),
            whole((width, columns)),
            whole((1, HEAD_SIZE)),
            whole((1, HEAD_SIZE)),
            pl.BlockSpec((rows, HEAD_SIZE), lambda i: (i, 0)),
            pl.BlockSpec((rows, HEAD_SIZE), lambda i: (i, 0)),
        ],
        out_specs=[
            pl.BlockSpec((width, rows), lambda i: (0, i)),
            pl.BlockSpec((rows, columns), lambda i: (i, 0)),
            pl.BlockSpec((rows, columns), lambda i: (i, 0)),
        ],
        out_shape=[
            jax.ShapeDtypeStruct((width, tokens), BF16),
            jax.ShapeDtypeStruct((tokens, columns), BF16),
            jax.ShapeDtypeStruct((tokens, columns), BF16),
        ],
        compiler_params=params("arbitrary"),
        name="project",
    )(x, gain, weights, query_norm, key_norm, cosine, sine)


BLOCK = 512


def split_three(values):
    lane = lax.broadcasted_iota(jnp.int32, values.shape, 1)
    high = values.astype(BF16).astype(F32)
    rest = values - high
    middle = rest.astype(BF16).astype(F32)
    low = rest - middle
    return jnp.where(
        lane == 0, high, jnp.where(lane == 1, middle, jnp.where(lane == 2, low, 0.0))
    ).astype(BF16)


def attend_kernel(first, q_ref, k_ref, v_ref, out_ref, log_ref, v_ones, acc):
    i = pl.program_id(1)

    @pl.when(i == 0)
    def _():
        v_ones[:, :HEAD_SIZE] = v_ref[...]
        v_ones[:, HEAD_SIZE:] = jnp.ones(v_ref.shape, BF16)

    acc[...] = jnp.zeros_like(acc)

    def tile(start, masked):
        keys = k_ref[pl.ds(start, BLOCK), :]
        values = v_ones[pl.ds(start, BLOCK), :]
        for head in range(2):
            s = nt(q_ref[:, head * HEAD_SIZE : (head + 1) * HEAD_SIZE], keys)
            if masked:
                row = lax.broadcasted_iota(jnp.int32, s.shape, 0)
                column = lax.broadcasted_iota(jnp.int32, s.shape, 1)
                s = jnp.where(column <= row, s, masked_score)
            acc[head] += nn(jnp.exp2(s).astype(BF16), values)

    def step(j, carry):
        tile(pl.multiple_of(j * BLOCK, BLOCK), False)
        return carry

    lax.fori_loop(0, i + first, step, 0)
    tile(pl.multiple_of((i + first) * BLOCK, BLOCK), True)
    for head in range(2):
        columns = slice(head * HEAD_SIZE, (head + 1) * HEAD_SIZE)
        total = acc[head, :, HEAD_SIZE:]
        out_ref[:, columns] = (acc[head, :, :HEAD_SIZE] / total).astype(BF16)
        log_ref[:, columns] = split_three(jnp.log(total) * (-1.0 / LN2))


def attend(rot, half):
    groups = rot.shape[1] // GROUP
    width = 2 * HEAD_SIZE
    blocks = HALF // BLOCK
    first = half * blocks
    keys = HALF * (half + 1)
    return pl.pallas_call(
        lambda *refs: attend_kernel(first, *refs),
        grid=(groups, blocks),
        in_specs=[
            pl.BlockSpec((BLOCK, width), lambda c, i: (i + first, 2 * c)),
            pl.BlockSpec((keys, HEAD_SIZE), lambda c, i: (0, 4 * c + 2)),
            pl.BlockSpec((keys, HEAD_SIZE), lambda c, i: (0, 4 * c + 3)),
        ],
        out_specs=[
            pl.BlockSpec((BLOCK, width), lambda c, i: (i, c)),
            pl.BlockSpec((BLOCK, width), lambda c, i: (i, c)),
        ],
        out_shape=[
            jax.ShapeDtypeStruct((HALF, groups * width), BF16),
            jax.ShapeDtypeStruct((HALF, groups * width), BF16),
        ],
        scratch_shapes=[
            pltpu.VMEM((keys, width), BF16),
            pltpu.VMEM((2, BLOCK, width), F32),
        ],
        compiler_params=params("arbitrary", "arbitrary"),
        name="attend",
    )(rot, rot, rot)


def out_project_kernel(mixed_ref, w_ref, out_ref):
    out_ref[...] = nt(mixed_ref[...], w_ref[...]).astype(BF16)


def out_project(mixed, weights):
    rows = 256
    width, heads = weights.shape[0], mixed.shape[1]
    return pl.pallas_call(
        out_project_kernel,
        grid=(HALF // rows,),
        in_specs=[
            pl.BlockSpec((rows, heads), lambda i: (i, 0)),
            out_weight_spec(width, heads),
        ],
        out_specs=pl.BlockSpec((rows, width), lambda i: (i, 0)),
        out_shape=jax.ShapeDtypeStruct((HALF, width), BF16),
        compiler_params=params("arbitrary"),
        name="out_project",
    )(mixed, weights)


ROWS = 256


def attend_back_kernel(
    rot_ref, raw_ref, do_a, do_b, out_a, out_b, log_a, log_b, qn_ref, kn_ref, cos_ref, sin_ref,
    bits_ref, qg_ref, kg_ref,
    q_wide, d_wide, k_wide, v_wide, k_flip, dq_flip, dk, dv,
):
    blocks = SEQ_LEN // BLOCK
    lane = lax.broadcasted_iota(jnp.int32, (ROWS, HEAD_SIZE), 1)
    ones = jnp.where(lane < 3, 1.0, 0.0).astype(BF16)

    def prepare(half, do_ref, out_ref, log_ref):
        def body(r, carry):
            near = pl.ds(pl.multiple_of(r * ROWS, ROWS), ROWS)
            rows = pl.ds(pl.multiple_of(half * HALF + r * ROWS, ROWS), ROWS)
            key = rot_ref[rows, 2 * HEAD_SIZE : 3 * HEAD_SIZE]
            k_wide[rows, :HEAD_SIZE] = key
            k_wide[rows, HEAD_SIZE:] = ones
            v_wide[rows, :HEAD_SIZE] = rot_ref[rows, 3 * HEAD_SIZE :]
            v_wide[rows, HEAD_SIZE:] = ones
            k_flip[:, rows] = key.T
            for head in range(2):
                columns = slice(head * HEAD_SIZE, (head + 1) * HEAD_SIZE)
                q_wide[head, rows, :HEAD_SIZE] = rot_ref[rows, columns]
                q_wide[head, rows, HEAD_SIZE:] = log_ref[near, columns]
                grad = do_ref[near, columns]
                delta = jnp.sum(
                    grad.astype(F32) * out_ref[near, columns].astype(F32), axis=-1, keepdims=True
                )
                d_wide[head, rows, :HEAD_SIZE] = grad
                d_wide[head, rows, HEAD_SIZE:] = split_three(
                    jnp.broadcast_to(-delta, (ROWS, HEAD_SIZE))
                )
            return carry

        lax.fori_loop(0, HALF // ROWS, body, 0)

    prepare(0, do_a, out_a, log_a)
    prepare(1, do_b, out_b, log_b)
    dq_flip[...] = jnp.zeros_like(dq_flip)

    def tile(kv, start, masked, first):
        q_rows = pl.ds(start, BLOCK)
        for head in range(2):
            q = q_wide[head, q_rows, :]
            d = d_wide[head, q_rows, :]
            s = nt(k_wide[kv, :], q)
            if masked:
                row = lax.broadcasted_iota(jnp.int32, s.shape, 0)
                column = lax.broadcasted_iota(jnp.int32, s.shape, 1)
                s = jnp.where(row <= column, s, masked_score)
            p = jnp.exp2(s)
            ds = (p * nt(v_wide[kv, :], d)).astype(BF16)
            new_dv = nn(p.astype(BF16), d[:, :HEAD_SIZE])
            new_dk = nn(ds, q[:, :HEAD_SIZE])
            if first and head == 0:
                dv[kv, :] = new_dv
                dk[kv, :] = new_dk
            else:
                dv[kv, :] += new_dv
                dk[kv, :] += new_dk
            dq_flip[head, :, q_rows] += nn(k_flip[:, kv], ds)

    def key_block(j, carry):
        start = pl.multiple_of(j * BLOCK, BLOCK)
        kv = pl.ds(start, BLOCK)
        tile(kv, start, True, True)

        def query_block(i, inner):
            tile(kv, pl.multiple_of(i * BLOCK, BLOCK), False, False)
            return inner

        return lax.fori_loop(j + 1, blocks, query_block, carry)

    lax.fori_loop(0, blocks, key_block, 0)

    qg_ref[...] = jnp.zeros_like(qg_ref)
    kg_ref[...] = jnp.zeros_like(kg_ref)

    def finish(r, carry):
        rows = pl.ds(pl.multiple_of(r * ROWS, ROWS), ROWS)
        cosine, sine = cos_ref[rows, :], sin_ref[rows, :]
        for head in range(3):
            columns = slice(head * HEAD_SIZE, (head + 1) * HEAD_SIZE)
            if head < 2:
                u = dq_flip[head, :, rows].T * LN2
                gain, total = qn_ref[...], qg_ref
            else:
                u = dk[rows, :] * SCORE_SCALE
                gain, total = kn_ref[...], kg_ref
            u = u * cosine - pltpu.roll(u, HEAD_SIZE // 2, 1) * sine
            x = raw_ref[rows, columns].astype(F32)
            scale = lax.rsqrt(jnp.mean(x * x, axis=-1, keepdims=True) + epsilon)
            x = x * scale
            total[0] += jnp.sum((u * x).reshape(ROWS // 8, 8, HEAD_SIZE), axis=0)
            w = u * gain
            bits_ref[rows, columns] = (
                scale * (w - x * jnp.mean(w * x, axis=-1, keepdims=True))
            ).astype(BF16)
        bits_ref[rows, 3 * HEAD_SIZE :] = dv[rows, :].astype(BF16)
        return carry

    lax.fori_loop(0, SEQ_LEN // ROWS, finish, 0)


def attend_back(rot, raw, grads, outs, logs, query_norm, key_norm, cosine, sine):
    groups = rot.shape[1] // GROUP
    width = 2 * HEAD_SIZE
    return pl.pallas_call(
        attend_back_kernel,
        grid=(groups,),
        in_specs=[
            pl.BlockSpec((SEQ_LEN, GROUP), lambda c: (0, c)),
            pl.BlockSpec((SEQ_LEN, GROUP), lambda c: (0, c)),
            *[pl.BlockSpec((HALF, width), lambda c: (0, c))] * 6,
            whole((1, HEAD_SIZE)),
            whole((1, HEAD_SIZE)),
            whole((SEQ_LEN, HEAD_SIZE)),
            whole((SEQ_LEN, HEAD_SIZE)),
        ],
        out_specs=[
            pl.BlockSpec((SEQ_LEN, GROUP), lambda c: (0, c)),
            pl.BlockSpec((1, 8, HEAD_SIZE), lambda c: (c, 0, 0)),
            pl.BlockSpec((1, 8, HEAD_SIZE), lambda c: (c, 0, 0)),
        ],
        out_shape=[
            jax.ShapeDtypeStruct((SEQ_LEN, groups * GROUP), BF16),
            jax.ShapeDtypeStruct((groups, 8, HEAD_SIZE), F32),
            jax.ShapeDtypeStruct((groups, 8, HEAD_SIZE), F32),
        ],
        scratch_shapes=[
            pltpu.VMEM((2, SEQ_LEN, width), BF16),
            pltpu.VMEM((2, SEQ_LEN, width), BF16),
            pltpu.VMEM((SEQ_LEN, width), BF16),
            pltpu.VMEM((SEQ_LEN, width), BF16),
            pltpu.VMEM((HEAD_SIZE, SEQ_LEN), BF16),
            pltpu.VMEM((2, HEAD_SIZE, SEQ_LEN), F32),
            pltpu.VMEM((SEQ_LEN, HEAD_SIZE), F32),
            pltpu.VMEM((SEQ_LEN, HEAD_SIZE), F32),
        ],
        compiler_params=params("arbitrary"),
        name="attend_back",
    )(rot, raw, *grads, *outs, *logs, query_norm, key_norm, cosine, sine)


def residual_of(x_ref, own_ref, other_ref):
    residual = x_ref[...].astype(F32) + (own_ref[...].astype(F32) + other_ref[...].astype(F32))
    scale = lax.rsqrt(jnp.mean(residual * residual, axis=-1, keepdims=True) + epsilon)
    return residual * scale, scale


def middle_kernel(
    x_ref, own_ref, other_ref, grad_ref, fn_ref, w_ref, down_ref, flip_ref, y_ref, fg_ref
):
    width, columns = w_ref.shape
    hidden = columns // 3
    chunk = 512 if hidden % 512 == 0 else hidden
    rows = x_ref.shape[0]
    normed, scale = residual_of(x_ref, own_ref, other_ref)
    f = (normed * fn_ref[...]).astype(BF16)
    grad = grad_ref[...]
    flip_ref[0] = f.T
    flip_ref[1] = grad.T
    total = jnp.zeros((rows, width), F32)
    f_grad = jnp.zeros((rows, width), F32)
    for start in range(0, hidden, chunk):
        gate_w = w_ref[:, start : start + chunk]
        up_w = w_ref[:, hidden + start : hidden + start + chunk]
        down_w = w_ref[:, 2 * hidden + start : 2 * hidden + start + chunk]
        gate, up = nn(f, gate_w), nn(f, up_w)
        sig = 1.0 / (1.0 + jnp.exp(-gate))
        silu = gate * sig
        low = (silu * up).astype(BF16)
        total += nt(low, down_w)
        hidden_grad = nn(grad, down_w)
        gate_bits = (hidden_grad * up * (sig * (1.0 + gate * (1.0 - sig)))).astype(BF16)
        up_bits = (hidden_grad * silu).astype(BF16)
        y_ref[:, start : start + chunk] = gate_bits
        y_ref[:, hidden + start : hidden + start + chunk] = up_bits
        y_ref[:, 2 * hidden + start : 2 * hidden + start + chunk] = low
        f_grad += nt(gate_bits, gate_w) + nt(up_bits, up_w)
    down_ref[...] = total.astype(BF16)
    fg_ref[...] = f_grad.astype(BF16)


def half_rows(rows, width, half):
    return pl.BlockSpec((rows, width), lambda i: (i + half * (HALF // rows), 0))


def middle(half, x_all, own, other, grad_all, gain, weights):
    width, columns = weights.shape
    rows = 256
    near = pl.BlockSpec((rows, width), lambda i: (i, 0))
    return pl.pallas_call(
        middle_kernel,
        grid=(HALF // rows,),
        in_specs=[
            half_rows(rows, width, half), near, near, half_rows(rows, width, half),
            whole((1, width)), whole(weights.shape),
        ],
        out_specs=[
            near,
            pl.BlockSpec((2, width, rows), lambda i: (0, 0, i)),
            pl.BlockSpec((rows, columns), lambda i: (i, 0)),
            near,
        ],
        out_shape=[
            jax.ShapeDtypeStruct((HALF, width), BF16),
            jax.ShapeDtypeStruct((2, width, HALF), BF16),
            jax.ShapeDtypeStruct((HALF, columns), BF16),
            jax.ShapeDtypeStruct((HALF, width), BF16),
        ],
        compiler_params=params("arbitrary"),
        name="middle",
    )(x_all, own, other, grad_all, gain, weights)


def residual_back_kernel(
    x_ref, own_ref, other_ref, grad_ref, fg_ref, fg_other_ref, fn_ref, w_ref,
    rg_ref, flip_ref, mg_ref, fng_ref,
):
    rows, width = x_ref.shape
    normed, scale = residual_of(x_ref, own_ref, other_ref)
    f_grad = fg_ref[...].astype(F32) + fg_other_ref[...].astype(F32)

    @pl.when(pl.program_id(0) == 0)
    def _():
        fng_ref[...] = jnp.zeros_like(fng_ref)

    fng_ref[...] += jnp.sum((f_grad * normed).reshape(rows // 8, 8, width), axis=0)
    u = f_grad * fn_ref[...]
    residual_grad = grad_ref[...].astype(F32) + scale * (
        u - normed * jnp.mean(u * normed, axis=-1, keepdims=True)
    )
    rg_ref[...] = residual_grad
    proj = residual_grad.astype(BF16)
    flip_ref[...] = proj.T
    mg_ref[...] = nn(proj, w_ref[...]).astype(BF16)


def residual_back(half, x_all, own, other, grad_all, fg, fg_other, gain, weights, heads):
    width = weights.shape[0]
    rows = 256
    near = pl.BlockSpec((rows, width), lambda i: (i, 0))
    return pl.pallas_call(
        residual_back_kernel,
        grid=(HALF // rows,),
        in_specs=[
            half_rows(rows, width, half), near, near, half_rows(rows, width, half), near, near,
            whole((1, width)), out_weight_spec(width, heads),
        ],
        out_specs=[
            near,
            pl.BlockSpec((width, rows), lambda i: (0, i)),
            pl.BlockSpec((rows, heads), lambda i: (i, 0)),
            pl.BlockSpec((8, width), lambda i: (0, 0)),
        ],
        out_shape=[
            jax.ShapeDtypeStruct((HALF, width), F32),
            jax.ShapeDtypeStruct((width, HALF), BF16),
            jax.ShapeDtypeStruct((HALF, heads), BF16),
            jax.ShapeDtypeStruct((8, width), F32),
        ],
        compiler_params=params("arbitrary"),
        name="residual_back",
    )(x_all, own, other, grad_all, fg, fg_other, gain, weights)


def middle_weights_kernel(bound, flip_a, flip_b, y_a, y_b, out_ref):
    which = jnp.where(pl.program_id(0) < bound, 0, 1)
    out_ref[...] = (nn(flip_a[which], y_a[...]) + nn(flip_b[which], y_b[...])).astype(BF16)


def middle_weights(flips, ys):
    width = flips[0].shape[1]
    columns = ys[0].shape[1]
    hidden = columns // 3
    size = 512 if hidden % 512 == 0 else hidden
    bound = 2 * hidden // size
    y_spec = pl.BlockSpec((HALF, size), lambda i: (0, i))
    return pl.pallas_call(
        lambda *refs: middle_weights_kernel(bound, *refs),
        grid=(columns // size,),
        in_specs=[whole(flips[0].shape), whole(flips[1].shape), y_spec, y_spec],
        out_specs=pl.BlockSpec((width, size), lambda i: (0, i)),
        out_shape=jax.ShapeDtypeStruct((width, columns), BF16),
        compiler_params=params("arbitrary"),
        name="middle_weights",
    )(*flips, *ys)


def attention_weights_kernel(
    bound, input_flip, proj_a, proj_b, bits_ref, mixed_a, mixed_b, w_ref, out_ref, sums_ref
):
    i = pl.program_id(0)

    @pl.when(i == 0)
    def _():
        sums_ref[...] = jnp.zeros_like(sums_ref)

    @pl.when(i < bound)
    def _():
        out = nn(input_flip[...], bits_ref[...])
        out_ref[...] = out.astype(BF16)
        product = out * w_ref[...].astype(F32)
        for start in range(0, product.shape[1], 128):
            sums_ref[...] += product[:, start : start + 128]

    @pl.when(i >= bound)
    def _():
        out_ref[...] = (nn(proj_a[...], mixed_a[...]) + nn(proj_b[...], mixed_b[...])).astype(BF16)


def attention_weights(input_flip, projs, bits, mixed, weights):
    width, columns = weights.shape
    heads = columns // 3
    size = math.gcd(512, heads)
    bound = 2 * heads // size
    mixed_spec = pl.BlockSpec((HALF, size), lambda i: (0, jnp.maximum(i - bound, 0)))
    return pl.pallas_call(
        lambda *refs: attention_weights_kernel(bound, *refs),
        grid=(columns // size,),
        in_specs=[
            whole(input_flip.shape), whole(projs[0].shape), whole(projs[1].shape),
            pl.BlockSpec((SEQ_LEN, size), lambda i: (0, jnp.minimum(i, bound - 1))),
            mixed_spec, mixed_spec,
            pl.BlockSpec((width, size), lambda i: (0, i)),
        ],
        out_specs=[
            pl.BlockSpec((width, size), lambda i: (0, i)),
            pl.BlockSpec((width, 128), lambda i: (0, 0)),
        ],
        out_shape=[
            jax.ShapeDtypeStruct((width, columns), BF16),
            jax.ShapeDtypeStruct((width, 128), F32),
        ],
        compiler_params=params("arbitrary"),
        name="attention_weights",
    )(input_flip, *projs, bits, *mixed, weights)


def input_back_kernel(place_ref, bits_ref, w_ref, out_ref):
    out_ref[...] = nt(bits_ref[...], w_ref[...]).astype(BF16)


def input_back(place, tokens, bits, weights):
    width = weights.shape[0]
    columns = bits.shape[1]
    rows = 256
    blocks = tokens // rows
    return pl.pallas_call(
        input_back_kernel,
        grid_spec=pltpu.PrefetchScalarGridSpec(
            num_scalar_prefetch=1,
            grid=(blocks,),
            in_specs=[
                pl.BlockSpec((rows, columns), lambda i, place: (place[0] * blocks + i, 0)),
                whole((width, columns)),
            ],
            out_specs=pl.BlockSpec((rows, width), lambda i, place: (i, 0)),
        ),
        out_shape=jax.ShapeDtypeStruct((tokens, width), BF16),
        compiler_params=params("arbitrary"),
        name="input_back",
    )(place.reshape(1), bits, weights)


def swap(values):
    return lax.ppermute(values, "tensor", [(0, 1), (1, 0)])


def in_order(own, other, axis):
    first = lax.axis_index("tensor") == 0
    return jnp.concatenate(
        [jnp.where(first, own, other), jnp.where(first, other, own)], axis=axis
    )


def gather_tokens(values, ranks):
    if ranks == 2:
        return in_order(values, swap(values), 0)
    return lax.all_gather(values, "tensor", axis=0, tiled=True)


def others_sum(values, ranks):
    if ranks == 2:
        return swap(values)
    own = values.astype(F32)
    return (lax.psum(own, "tensor") - own).astype(BF16)


def own_rows(halves, ranks, me, rows):
    if ranks == 2:
        return jnp.where(me == 0, halves[0], halves[1])
    return lax.dynamic_slice_in_dim(jnp.concatenate(halves, axis=0), me * rows, rows)


def after(values, *events):
    return lax.optimization_barrier((values, *events))[0]


def on_device(
    layer_input,
    attention_norm,
    query_weight,
    key_matrix,
    value_matrix,
    query_norm,
    key_norm,
    output_weight,
    feedforward_norm,
    gate_weight,
    up_weight,
    down_weight,
    out_grad,
):
    ranks = lax.axis_size("tensor")
    me = lax.axis_index("tensor")
    depth = query_weight.shape[0]
    tok_rows, width = layer_input.shape
    groups = key_matrix.shape[1] // HEAD_SIZE
    heads = query_weight.shape[1]
    hidden = gate_weight.shape[1]

    own_attention = jnp.concatenate(
        [
            jnp.concatenate(
                [
                    query_weight.reshape(depth, groups, 2 * HEAD_SIZE),
                    key_matrix.reshape(depth, groups, HEAD_SIZE),
                    value_matrix.reshape(depth, groups, HEAD_SIZE),
                ],
                axis=2,
            ).reshape(depth, groups * GROUP),
            output_weight.T,
        ],
        axis=1,
    )
    attention_w = lax.all_gather(own_attention, "dp", axis=0, tiled=True)
    x_all = gather_tokens(layer_input, ranks)
    own_middle = jnp.concatenate([gate_weight, up_weight, down_weight.T], axis=1)
    middle_w = lax.all_gather(own_middle, "dp", axis=0, tiled=True)
    grad_all = gather_tokens(after(out_grad, x_all), ranks)

    cosine, sine = rope_tables()
    norm_q, norm_k = query_norm[None, :], key_norm[None, :]
    norm_two = feedforward_norm[None, :]
    input_flip, raw, rot = project(
        x_all, attention_norm[None, :], attention_w, norm_q, norm_k, cosine, sine
    )
    mixed, logs, owns, others = [], [], [], []
    for half in range(2):
        out, log = attend(after(rot, *owns), half)
        mixed.append(out)
        logs.append(log)
        owns.append(out_project(out, attention_w))
        others.append(others_sum(owns[half], ranks))

    downs, flips, ys, f_grads, f_others = [], [], [], [], []
    for half in range(2):
        down, flip, y, f_grad = middle(
            half, x_all, owns[half], others[half], grad_all, norm_two, middle_w
        )
        downs.append(down)
        flips.append(flip)
        ys.append(y)
        f_grads.append(f_grad)
        f_others.append(others_sum(f_grad, ranks))
    middle_part = middle_weights(flips, ys)
    middle_grad = lax.psum_scatter(
        middle_part, "dp", scatter_dimension=0, tiled=True
    ).astype(F32)

    f_others[1] = after(f_others[1], middle_part)

    residual_grads, projs, mixed_grads, norm_two_part = [], [], [], 0.0
    for half in range(2):
        residual_grad, proj, mixed_grad, part = residual_back(
            half, x_all, owns[half], others[half], grad_all, f_grads[half], f_others[half],
            norm_two, attention_w, heads,
        )
        residual_grads.append(residual_grad)
        projs.append(proj)
        mixed_grads.append(mixed_grad)
        norm_two_part = norm_two_part + jnp.sum(part, axis=0) / ranks

    bits, query_part, key_part = attend_back(
        rot, raw, mixed_grads, mixed, logs, norm_q, norm_k, cosine, sine
    )

    if ranks == 2:
        send = after(jnp.where(me == 0, downs[1], downs[0]), mixed_grads[1])
        down_sum = own_rows(downs, ranks, me, tok_rows).astype(F32) + swap(send).astype(F32)
    else:
        down_sum = lax.psum_scatter(
            jnp.concatenate(downs, axis=0).astype(F32), "tensor", scatter_dimension=0, tiled=True
        )
    x = layer_input.astype(F32)
    residual = x + (
        own_rows(owns, ranks, me, tok_rows).astype(F32)
        + own_rows(others, ranks, me, tok_rows).astype(F32)
    )
    layer_output = (residual + down_sum).astype(BF16)

    attention_part, sums = attention_weights(input_flip, projs, bits, mixed, attention_w)
    attention_grad = lax.psum_scatter(
        attention_part, "dp", scatter_dimension=0, tiled=True
    ).astype(F32)
    norm_one_part = jnp.sum(sums, axis=1) / attention_norm
    if ranks == 2:
        other = swap(input_back(1 - me, tok_rows, bits, attention_w))
        own = input_back(me, tok_rows, bits, attention_w)
        attention_input_grad = own.astype(F32) + other.astype(F32)
    else:
        attention_input_grad = lax.psum_scatter(
            input_back(jnp.zeros_like(me), SEQ_LEN, bits, attention_w).astype(F32),
            "tensor",
            scatter_dimension=0,
            tiled=True,
        )
    scale = lax.rsqrt(jnp.mean(x * x, axis=-1, keepdims=True) + epsilon)
    normed = x * scale
    u = attention_input_grad * attention_norm
    input_grad = own_rows(residual_grads, ranks, me, tok_rows) + scale * (
        u - normed * jnp.mean(u * normed, axis=-1, keepdims=True)
    )
    attention_norm_grad, feedforward_norm_grad, query_norm_grad, key_norm_grad = lax.psum(
        (
            norm_one_part,
            norm_two_part,
            jnp.sum(query_part, axis=(0, 1)),
            jnp.sum(key_part, axis=(0, 1)),
        ),
        ("dp", "tensor"),
    )
    qkv_grad = attention_grad[:, : groups * GROUP].reshape(depth, groups, GROUP)
    return (
        layer_output,
        input_grad,
        attention_norm_grad,
        qkv_grad[:, :, : 2 * HEAD_SIZE].reshape(depth, -1),
        qkv_grad[:, :, 2 * HEAD_SIZE : 3 * HEAD_SIZE].reshape(depth, -1),
        qkv_grad[:, :, 3 * HEAD_SIZE :].reshape(depth, -1),
        query_norm_grad,
        key_norm_grad,
        attention_grad[:, groups * GROUP :].T,
        feedforward_norm_grad,
        middle_grad[:, :hidden],
        middle_grad[:, hidden : 2 * hidden],
        middle_grad[:, 2 * hidden :].T,
    )


def solution(mesh):
    return jax.shard_map(
        on_device,
        mesh=mesh,
        in_specs=(
            P(("dp", "tensor"), None),
            P(),
            P("dp", "tensor"),
            P("dp", "tensor"),
            P("dp", "tensor"),
            P(),
            P(),
            P("tensor", "dp"),
            P(),
            P("dp", "tensor"),
            P("dp", "tensor"),
            P("tensor", "dp"),
            P(("dp", "tensor"), None),
        ),
        out_specs=(
            P(("dp", "tensor"), None),
            P(("dp", "tensor"), None),
            P(),
            P("dp", "tensor"),
            P("dp", "tensor"),
            P("dp", "tensor"),
            P(),
            P(),
            P("tensor", "dp"),
            P(),
            P("dp", "tensor"),
            P("dp", "tensor"),
            P("tensor", "dp"),
        ),
        check_vma=False,
    )
```

```python
import math

import jax
import jax.numpy as jnp
from jax import lax
from jax.experimental import pallas as pl
from jax.experimental.pallas import tpu as pltpu
from jax.sharding import PartitionSpec as P

HEAD_SIZE = 128
SEQ_LEN = 2048

epsilon = 1e-06
rope_base = 1000000.0
masked_score = -1e30
LN2 = math.log(2.0)
SCORE_SCALE = HEAD_SIZE ** (-0.5)
GROUP = 4 * HEAD_SIZE
F32 = jnp.float32
BF16 = jnp.bfloat16
VMEM_LIMIT = 60 * 1024 * 1024
HALF = SEQ_LEN // 2


def nn(left, right):
    return lax.dot_general(left, right, (((1,), (0,)), ((), ())), preferred_element_type=F32)


def nt(left, right):
    return lax.dot_general(left, right, (((1,), (1,)), ((), ())), preferred_element_type=F32)


def rope_tables():
    position = jnp.arange(SEQ_LEN).astype(F32)
    inverse = jnp.power(rope_base, -jnp.arange(HEAD_SIZE // 2).astype(F32) * (2.0 / HEAD_SIZE))
    angles = position[:, None] * inverse[None, :]
    cosine, sine = jnp.cos(angles), jnp.sin(angles)
    return (
        jnp.concatenate([cosine, cosine], axis=1),
        jnp.concatenate([-sine, sine], axis=1),
    )


def params(*semantics):
    return pltpu.CompilerParams(dimension_semantics=semantics, vmem_limit_bytes=VMEM_LIMIT)


def cost(flops, rate):
    return pl.CostEstimate(flops=int(flops * (1000.0 / rate)), bytes_accessed=0, transcendentals=0)


def whole(shape):
    return pl.BlockSpec(shape, lambda *_: (0,) * len(shape), pipeline_mode=pl.Buffered(1))


def out_weight_spec(width, heads):
    return pl.BlockSpec((width, heads), lambda *_: (0, 2), pipeline_mode=pl.Buffered(1))


def project_kernel(x_ref, gain_ref, w_ref, qn_ref, kn_ref, cos_ref, sin_ref, at_ref, raw_ref, rot_ref):
    x = x_ref[...].astype(F32)
    scale = lax.rsqrt(jnp.mean(x * x, axis=-1, keepdims=True) + epsilon)
    a = (x * scale * gain_ref[...]).astype(BF16)
    at_ref[...] = a.T
    cosine, sine = cos_ref[...], sin_ref[...]
    for group in range(w_ref.shape[1] // GROUP):
        base = group * GROUP
        y = nn(a, w_ref[:, base : base + GROUP])
        raw_ref[:, base : base + GROUP] = y.astype(BF16)
        for head in range(3):
            z = y[:, head * HEAD_SIZE : (head + 1) * HEAD_SIZE]
            gain = kn_ref[...] * (SCORE_SCALE / LN2) if head == 2 else qn_ref[...]
            z = z * lax.rsqrt(jnp.mean(z * z, axis=-1, keepdims=True) + epsilon) * gain
            z = z * cosine + pltpu.roll(z, HEAD_SIZE // 2, 1) * sine
            rot_ref[:, base + head * HEAD_SIZE : base + (head + 1) * HEAD_SIZE] = z.astype(BF16)
        rot_ref[:, base + 3 * HEAD_SIZE : base + GROUP] = y[:, 3 * HEAD_SIZE :].astype(BF16)


def project(x, gain, weights, query_norm, key_norm, cosine, sine):
    tokens, width = x.shape
    columns = weights.shape[1] // 3 * 2
    rows = 256
    return pl.pallas_call(
        project_kernel,
        grid=(tokens // rows,),
        in_specs=[
            pl.BlockSpec((rows, width), lambda i: (i, 0)),
            whole((1, width)),
            whole((width, columns)),
            whole((1, HEAD_SIZE)),
            whole((1, HEAD_SIZE)),
            pl.BlockSpec((rows, HEAD_SIZE), lambda i: (i, 0)),
            pl.BlockSpec((rows, HEAD_SIZE), lambda i: (i, 0)),
        ],
        out_specs=[
            pl.BlockSpec((width, rows), lambda i: (0, i)),
            pl.BlockSpec((rows, columns), lambda i: (i, 0)),
            pl.BlockSpec((rows, columns), lambda i: (i, 0)),
        ],
        out_shape=[
            jax.ShapeDtypeStruct((width, tokens), BF16),
            jax.ShapeDtypeStruct((tokens, columns), BF16),
            jax.ShapeDtypeStruct((tokens, columns), BF16),
        ],
        compiler_params=params("arbitrary"),
        cost_estimate=cost(2 * tokens * width * columns, 500),
        name="project",
    )(x, gain, weights, query_norm, key_norm, cosine, sine)


BLOCK = 512


def split_three(values):
    lane = lax.broadcasted_iota(jnp.int32, values.shape, 1)
    high = values.astype(BF16).astype(F32)
    rest = values - high
    middle = rest.astype(BF16).astype(F32)
    low = rest - middle
    return jnp.where(
        lane == 0, high, jnp.where(lane == 1, middle, jnp.where(lane == 2, low, 0.0))
    ).astype(BF16)


def attend_kernel(first, q_ref, k_ref, v_ref, out_ref, log_ref, v_ones, acc):
    i = pl.program_id(1)

    @pl.when(i == 0)
    def _():
        v_ones[:, :HEAD_SIZE] = v_ref[...]
        v_ones[:, HEAD_SIZE:] = jnp.ones(v_ref.shape, BF16)

    acc[...] = jnp.zeros_like(acc)

    def tile(row, rows, start, size, masked):
        keys = k_ref[pl.ds(start, size), :]
        values = v_ones[pl.ds(start, size), :]
        for head in range(2):
            s = nt(q_ref[row : row + rows, head * HEAD_SIZE : (head + 1) * HEAD_SIZE], keys)
            if masked:
                query = lax.broadcasted_iota(jnp.int32, s.shape, 0)
                key = lax.broadcasted_iota(jnp.int32, s.shape, 1)
                s = jnp.where(key <= query + (size - rows), s, masked_score)
            acc[head, row : row + rows] += nn(jnp.exp2(s).astype(BF16), values)

    def step(j, carry):
        tile(0, BLOCK, pl.multiple_of(j * BLOCK, BLOCK), BLOCK, False)
        return carry

    lax.fori_loop(0, i + first, step, 0)
    start = pl.multiple_of((i + first) * BLOCK, BLOCK)
    tile(0, BLOCK // 2, start, BLOCK // 2, True)
    tile(BLOCK // 2, BLOCK // 2, start, BLOCK, True)
    for head in range(2):
        columns = slice(head * HEAD_SIZE, (head + 1) * HEAD_SIZE)
        total = acc[head, :, HEAD_SIZE:]
        out_ref[:, columns] = (acc[head, :, :HEAD_SIZE] / total).astype(BF16)
        log_ref[:, columns] = split_three(jnp.log(total) * (-1.0 / LN2))


def attend(rot, half):
    groups = rot.shape[1] // GROUP
    width = 2 * HEAD_SIZE
    blocks = HALF // BLOCK
    first = half * blocks
    keys = HALF * (half + 1)
    return pl.pallas_call(
        lambda *refs: attend_kernel(first, *refs),
        grid=(groups, blocks),
        in_specs=[
            pl.BlockSpec((BLOCK, width), lambda c, i: (i + first, 2 * c)),
            pl.BlockSpec((keys, HEAD_SIZE), lambda c, i: (0, 4 * c + 2)),
            pl.BlockSpec((keys, HEAD_SIZE), lambda c, i: (0, 4 * c + 3)),
        ],
        out_specs=[
            pl.BlockSpec((BLOCK, width), lambda c, i: (i, c)),
            pl.BlockSpec((BLOCK, width), lambda c, i: (i, c)),
        ],
        out_shape=[
            jax.ShapeDtypeStruct((HALF, groups * width), BF16),
            jax.ShapeDtypeStruct((HALF, groups * width), BF16),
        ],
        scratch_shapes=[
            pltpu.VMEM((keys, width), BF16),
            pltpu.VMEM((2, BLOCK, width), F32),
        ],
        compiler_params=params("arbitrary", "arbitrary"),
        cost_estimate=cost(4 * HALF * keys * groups * width, 500),
        name="attend",
    )(rot, rot, rot)


def out_project_kernel(mixed_ref, w_ref, out_ref):
    out_ref[...] = nt(mixed_ref[...], w_ref[...]).astype(BF16)


def out_project(mixed, weights):
    rows = 256
    width, heads = weights.shape[0], mixed.shape[1]
    return pl.pallas_call(
        out_project_kernel,
        grid=(HALF // rows,),
        in_specs=[
            pl.BlockSpec((rows, heads), lambda i: (i, 0)),
            out_weight_spec(width, heads),
        ],
        out_specs=pl.BlockSpec((rows, width), lambda i: (i, 0)),
        out_shape=jax.ShapeDtypeStruct((HALF, width), BF16),
        compiler_params=params("arbitrary"),
        cost_estimate=cost(2 * HALF * width * heads, 350),
        name="out_project",
    )(mixed, weights)


ROWS = 256


def attend_back_kernel(
    rot_ref, raw_ref, do_a, do_b, out_a, out_b, log_a, log_b, qn_ref, kn_ref, cos_ref, sin_ref,
    bits_ref, qg_ref, kg_ref,
    q_wide, d_wide, k_wide, v_wide, k_flip, dq_flip, dk, dv,
):
    blocks = SEQ_LEN // BLOCK
    lane = lax.broadcasted_iota(jnp.int32, (ROWS, HEAD_SIZE), 1)
    ones = jnp.where(lane < 3, 1.0, 0.0).astype(BF16)

    def prepare(half, do_ref, out_ref, log_ref):
        def body(r, carry):
            near = pl.ds(pl.multiple_of(r * ROWS, ROWS), ROWS)
            rows = pl.ds(pl.multiple_of(half * HALF + r * ROWS, ROWS), ROWS)
            key = rot_ref[rows, 2 * HEAD_SIZE : 3 * HEAD_SIZE]
            k_wide[rows, :HEAD_SIZE] = key
            k_wide[rows, HEAD_SIZE:] = ones
            v_wide[rows, :HEAD_SIZE] = rot_ref[rows, 3 * HEAD_SIZE :]
            v_wide[rows, HEAD_SIZE:] = ones
            k_flip[:, rows] = key.T
            for head in range(2):
                columns = slice(head * HEAD_SIZE, (head + 1) * HEAD_SIZE)
                q_wide[head, rows, :HEAD_SIZE] = rot_ref[rows, columns]
                q_wide[head, rows, HEAD_SIZE:] = log_ref[near, columns]
                grad = do_ref[near, columns]
                delta = jnp.sum(
                    grad.astype(F32) * out_ref[near, columns].astype(F32), axis=-1, keepdims=True
                )
                d_wide[head, rows, :HEAD_SIZE] = grad
                d_wide[head, rows, HEAD_SIZE:] = split_three(
                    jnp.broadcast_to(-delta, (ROWS, HEAD_SIZE))
                )
            return carry

        lax.fori_loop(0, HALF // ROWS, body, 0)

    prepare(0, do_a, out_a, log_a)
    prepare(1, do_b, out_b, log_b)
    dq_flip[...] = jnp.zeros_like(dq_flip)

    def tile(kv_start, kv_size, start, size, masked):
        kv, q_rows = pl.ds(kv_start, kv_size), pl.ds(start, size)
        for head in range(2):
            q = q_wide[head, q_rows, :]
            d = d_wide[head, q_rows, :]
            s = nt(k_wide[kv, :], q)
            if masked:
                row = lax.broadcasted_iota(jnp.int32, s.shape, 0)
                column = lax.broadcasted_iota(jnp.int32, s.shape, 1)
                s = jnp.where(row <= column, s, masked_score)
            p = jnp.exp2(s)
            ds = (p * nt(v_wide[kv, :], d)).astype(BF16)
            new_dv = nn(p.astype(BF16), d[:, :HEAD_SIZE])
            new_dk = nn(ds, q[:, :HEAD_SIZE])
            if masked and head == 0:
                dv[kv, :] = new_dv
                dk[kv, :] = new_dk
            else:
                dv[kv, :] += new_dv
                dk[kv, :] += new_dk
            dq_flip[head, :, q_rows] += nn(k_flip[:, kv], ds)

    part = BLOCK // 2

    def key_block(j, carry):
        start = pl.multiple_of(j * BLOCK, BLOCK)
        later = pl.multiple_of(j * BLOCK + part, part)
        tile(start, part, start, BLOCK, True)
        tile(later, part, later, part, True)

        def query_block(i, inner):
            tile(start, BLOCK, pl.multiple_of(i * BLOCK, BLOCK), BLOCK, False)
            return inner

        return lax.fori_loop(j + 1, blocks, query_block, carry)

    lax.fori_loop(0, blocks, key_block, 0)

    qg_ref[...] = jnp.zeros_like(qg_ref)
    kg_ref[...] = jnp.zeros_like(kg_ref)

    def finish(r, carry):
        rows = pl.ds(pl.multiple_of(r * ROWS, ROWS), ROWS)
        cosine, sine = cos_ref[rows, :], sin_ref[rows, :]
        for head in range(3):
            columns = slice(head * HEAD_SIZE, (head + 1) * HEAD_SIZE)
            if head < 2:
                u = dq_flip[head, :, rows].T * LN2
                gain, total = qn_ref[...], qg_ref
            else:
                u = dk[rows, :] * SCORE_SCALE
                gain, total = kn_ref[...], kg_ref
            u = u * cosine - pltpu.roll(u, HEAD_SIZE // 2, 1) * sine
            x = raw_ref[rows, columns].astype(F32)
            scale = lax.rsqrt(jnp.mean(x * x, axis=-1, keepdims=True) + epsilon)
            x = x * scale
            total[0] += jnp.sum((u * x).reshape(ROWS // 8, 8, HEAD_SIZE), axis=0)
            w = u * gain
            bits_ref[rows, columns] = (
                scale * (w - x * jnp.mean(w * x, axis=-1, keepdims=True))
            ).astype(BF16)
        bits_ref[rows, 3 * HEAD_SIZE :] = dv[rows, :].astype(BF16)
        return carry

    lax.fori_loop(0, SEQ_LEN // ROWS, finish, 0)


def attend_back(rot, raw, grads, outs, logs, query_norm, key_norm, cosine, sine):
    groups = rot.shape[1] // GROUP
    width = 2 * HEAD_SIZE
    return pl.pallas_call(
        attend_back_kernel,
        grid=(groups,),
        in_specs=[
            pl.BlockSpec((SEQ_LEN, GROUP), lambda c: (0, c)),
            pl.BlockSpec((SEQ_LEN, GROUP), lambda c: (0, c)),
            *[pl.BlockSpec((HALF, width), lambda c: (0, c))] * 6,
            whole((1, HEAD_SIZE)),
            whole((1, HEAD_SIZE)),
            whole((SEQ_LEN, HEAD_SIZE)),
            whole((SEQ_LEN, HEAD_SIZE)),
        ],
        out_specs=[
            pl.BlockSpec((SEQ_LEN, GROUP), lambda c: (0, c)),
            pl.BlockSpec((1, 8, HEAD_SIZE), lambda c: (c, 0, 0)),
            pl.BlockSpec((1, 8, HEAD_SIZE), lambda c: (c, 0, 0)),
        ],
        out_shape=[
            jax.ShapeDtypeStruct((SEQ_LEN, groups * GROUP), BF16),
            jax.ShapeDtypeStruct((groups, 8, HEAD_SIZE), F32),
            jax.ShapeDtypeStruct((groups, 8, HEAD_SIZE), F32),
        ],
        scratch_shapes=[
            pltpu.VMEM((2, SEQ_LEN, width), BF16),
            pltpu.VMEM((2, SEQ_LEN, width), BF16),
            pltpu.VMEM((SEQ_LEN, width), BF16),
            pltpu.VMEM((SEQ_LEN, width), BF16),
            pltpu.VMEM((HEAD_SIZE, SEQ_LEN), BF16),
            pltpu.VMEM((2, HEAD_SIZE, SEQ_LEN), F32),
            pltpu.VMEM((SEQ_LEN, HEAD_SIZE), F32),
            pltpu.VMEM((SEQ_LEN, HEAD_SIZE), F32),
        ],
        compiler_params=params("arbitrary"),
        cost_estimate=cost(5 * SEQ_LEN * SEQ_LEN * groups * width, 80),
        name="attend_back",
    )(rot, raw, *grads, *outs, *logs, query_norm, key_norm, cosine, sine)


def residual_of(x_ref, own_ref, other_ref):
    residual = x_ref[...].astype(F32) + (own_ref[...].astype(F32) + other_ref[...].astype(F32))
    scale = lax.rsqrt(jnp.mean(residual * residual, axis=-1, keepdims=True) + epsilon)
    return residual * scale, scale


def middle_kernel(
    x_ref, own_ref, other_ref, grad_ref, fn_ref, w_ref, down_ref, flip_ref, y_ref, fg_ref
):
    width, columns = w_ref.shape
    hidden = columns // 3
    chunk = 512 if hidden % 512 == 0 else hidden
    rows = x_ref.shape[0]
    normed, scale = residual_of(x_ref, own_ref, other_ref)
    f = (normed * fn_ref[...]).astype(BF16)
    grad = grad_ref[...]
    flip_ref[0] = f.T
    flip_ref[1] = grad.T
    total = jnp.zeros((rows, width), F32)
    f_grad = jnp.zeros((rows, width), F32)
    for start in range(0, hidden, chunk):
        gate_w = w_ref[:, start : start + chunk]
        up_w = w_ref[:, hidden + start : hidden + start + chunk]
        down_w = w_ref[:, 2 * hidden + start : 2 * hidden + start + chunk]
        gate, up = nn(f, gate_w), nn(f, up_w)
        sig = 1.0 / (1.0 + jnp.exp(-gate))
        silu = gate * sig
        low = (silu * up).astype(BF16)
        total += nt(low, down_w)
        hidden_grad = nn(grad, down_w)
        gate_bits = (hidden_grad * up * (sig * (1.0 + gate * (1.0 - sig)))).astype(BF16)
        up_bits = (hidden_grad * silu).astype(BF16)
        y_ref[:, start : start + chunk] = gate_bits
        y_ref[:, hidden + start : hidden + start + chunk] = up_bits
        y_ref[:, 2 * hidden + start : 2 * hidden + start + chunk] = low
        f_grad += nt(gate_bits, gate_w) + nt(up_bits, up_w)
    down_ref[...] = total.astype(BF16)
    fg_ref[...] = f_grad.astype(BF16)


def half_rows(rows, width, half):
    return pl.BlockSpec((rows, width), lambda i: (i + half * (HALF // rows), 0))


def middle(half, x_all, own, other, grad_all, gain, weights):
    width, columns = weights.shape
    rows = 256
    near = pl.BlockSpec((rows, width), lambda i: (i, 0))
    return pl.pallas_call(
        middle_kernel,
        grid=(HALF // rows,),
        in_specs=[
            half_rows(rows, width, half), near, near, half_rows(rows, width, half),
            whole((1, width)), whole(weights.shape),
        ],
        out_specs=[
            near,
            pl.BlockSpec((2, width, rows), lambda i: (0, 0, i)),
            pl.BlockSpec((rows, columns), lambda i: (i, 0)),
            near,
        ],
        out_shape=[
            jax.ShapeDtypeStruct((HALF, width), BF16),
            jax.ShapeDtypeStruct((2, width, HALF), BF16),
            jax.ShapeDtypeStruct((HALF, columns), BF16),
            jax.ShapeDtypeStruct((HALF, width), BF16),
        ],
        compiler_params=params("arbitrary"),
        cost_estimate=cost(4 * HALF * width * columns, 2500),
        name="middle",
    )(x_all, own, other, grad_all, gain, weights)


def residual_back_kernel(
    x_ref, own_ref, other_ref, grad_ref, fg_ref, fg_other_ref, fn_ref, w_ref,
    rg_ref, flip_ref, mg_ref, fng_ref,
):
    rows, width = x_ref.shape
    normed, scale = residual_of(x_ref, own_ref, other_ref)
    f_grad = fg_ref[...].astype(F32) + fg_other_ref[...].astype(F32)

    @pl.when(pl.program_id(0) == 0)
    def _():
        fng_ref[...] = jnp.zeros_like(fng_ref)

    fng_ref[...] += jnp.sum((f_grad * normed).reshape(rows // 8, 8, width), axis=0)
    u = f_grad * fn_ref[...]
    residual_grad = grad_ref[...].astype(F32) + scale * (
        u - normed * jnp.mean(u * normed, axis=-1, keepdims=True)
    )
    rg_ref[...] = residual_grad
    proj = residual_grad.astype(BF16)
    flip_ref[...] = proj.T
    mg_ref[...] = nn(proj, w_ref[...]).astype(BF16)


def residual_back(half, x_all, own, other, grad_all, fg, fg_other, gain, weights, heads):
    width = weights.shape[0]
    rows = 256
    near = pl.BlockSpec((rows, width), lambda i: (i, 0))
    return pl.pallas_call(
        residual_back_kernel,
        grid=(HALF // rows,),
        in_specs=[
            half_rows(rows, width, half), near, near, half_rows(rows, width, half), near, near,
            whole((1, width)), out_weight_spec(width, heads),
        ],
        out_specs=[
            near,
            pl.BlockSpec((width, rows), lambda i: (0, i)),
            pl.BlockSpec((rows, heads), lambda i: (i, 0)),
            pl.BlockSpec((8, width), lambda i: (0, 0)),
        ],
        out_shape=[
            jax.ShapeDtypeStruct((HALF, width), F32),
            jax.ShapeDtypeStruct((width, HALF), BF16),
            jax.ShapeDtypeStruct((HALF, heads), BF16),
            jax.ShapeDtypeStruct((8, width), F32),
        ],
        compiler_params=params("arbitrary"),
        cost_estimate=cost(2 * HALF * width * heads, 190),
        name="residual_back",
    )(x_all, own, other, grad_all, fg, fg_other, gain, weights)


def middle_weights_kernel(which, flip_a, flip_b, y_a, y_b, *rest):
    rest[-1][...] = (nn(flip_a[which], y_a[...]) + nn(flip_b[which], y_b[...])).astype(BF16)


def middle_weights(flips, ys, down, *partial):
    width = flips[0].shape[1]
    columns = ys[0].shape[1]
    hidden = columns // 3
    size = 512 if hidden % 512 == 0 else hidden
    bound = 2 * hidden // size
    first, blocks = (bound, columns // size - bound) if down else (0, bound)
    which = 1 if down else 0
    spec = pl.BlockSpec((HALF, size), lambda i: (0, i + first))
    flip_spec = pl.BlockSpec(
        (1, width, HALF), lambda i: (which, 0, 0), pipeline_mode=pl.Buffered(1)
    )
    return pl.pallas_call(
        lambda *refs: middle_weights_kernel(0, *refs),
        grid=(blocks,),
        in_specs=[flip_spec, flip_spec, spec, spec] + [pl.BlockSpec(memory_space=pl.ANY)] * len(partial),
        out_specs=pl.BlockSpec((width, size), lambda i: (0, i + first)),
        out_shape=jax.ShapeDtypeStruct((width, columns), BF16),
        input_output_aliases={4: 0} if partial else {},
        compiler_params=params("arbitrary"),
        cost_estimate=cost(2 * SEQ_LEN * width * size * blocks, 3000),
        name="down_weights" if down else "gate_up_weights",
    )(*flips, *ys, *partial)


def attention_weights_kernel(
    bound, input_flip, proj_a, proj_b, bits_ref, mixed_a, mixed_b, w_ref, out_ref, sums_ref
):
    i = pl.program_id(0)

    @pl.when(i == 0)
    def _():
        sums_ref[...] = jnp.zeros_like(sums_ref)

    @pl.when(i < bound)
    def _():
        out = nn(input_flip[...], bits_ref[...])
        out_ref[...] = out.astype(BF16)
        product = out * w_ref[...].astype(F32)
        for start in range(0, product.shape[1], 128):
            sums_ref[...] += product[:, start : start + 128]

    @pl.when(i >= bound)
    def _():
        out_ref[...] = (nn(proj_a[...], mixed_a[...]) + nn(proj_b[...], mixed_b[...])).astype(BF16)


def attention_weights(input_flip, projs, bits, mixed, weights):
    width, columns = weights.shape
    heads = columns // 3
    size = math.gcd(512, heads)
    bound = 2 * heads // size
    mixed_spec = pl.BlockSpec((HALF, size), lambda i: (0, jnp.maximum(i - bound, 0)))
    return pl.pallas_call(
        lambda *refs: attention_weights_kernel(bound, *refs),
        grid=(columns // size,),
        in_specs=[
            whole(input_flip.shape), whole(projs[0].shape), whole(projs[1].shape),
            pl.BlockSpec((SEQ_LEN, size), lambda i: (0, jnp.minimum(i, bound - 1))),
            mixed_spec, mixed_spec,
            pl.BlockSpec((width, size), lambda i: (0, i)),
        ],
        out_specs=[
            pl.BlockSpec((width, size), lambda i: (0, i)),
            pl.BlockSpec((width, 128), lambda i: (0, 0)),
        ],
        out_shape=[
            jax.ShapeDtypeStruct((width, columns), BF16),
            jax.ShapeDtypeStruct((width, 128), F32),
        ],
        compiler_params=params("arbitrary"),
        cost_estimate=cost(2 * SEQ_LEN * width * columns, 640),
        name="attention_weights",
    )(input_flip, *projs, bits, *mixed, weights)


def input_back_kernel(place_ref, bits_ref, w_ref, out_ref):
    out_ref[...] = nt(bits_ref[...], w_ref[...]).astype(BF16)


def input_back(place, tokens, bits, weights):
    width = weights.shape[0]
    columns = bits.shape[1]
    rows = 256
    blocks = tokens // rows
    return pl.pallas_call(
        input_back_kernel,
        grid_spec=pltpu.PrefetchScalarGridSpec(
            num_scalar_prefetch=1,
            grid=(blocks,),
            in_specs=[
                pl.BlockSpec((rows, columns), lambda i, place: (place[0] * blocks + i, 0)),
                whole((width, columns)),
            ],
            out_specs=pl.BlockSpec((rows, width), lambda i, place: (i, 0)),
        ),
        out_shape=jax.ShapeDtypeStruct((tokens, width), BF16),
        compiler_params=params("arbitrary"),
        cost_estimate=cost(2 * tokens * width * columns, 480),
        name="input_back",
    )(place.reshape(1), bits, weights)


def swap(values):
    return lax.ppermute(values, "tensor", [(0, 1), (1, 0)])


def in_order(own, other, axis):
    first = lax.axis_index("tensor") == 0
    return jnp.concatenate(
        [jnp.where(first, own, other), jnp.where(first, other, own)], axis=axis
    )


def send_tokens(values, ranks):
    if ranks == 2:
        return swap(values)
    return lax.all_gather(values, "tensor", axis=0, tiled=True)


def all_tokens(own, sent, ranks):
    return in_order(own, sent, 0) if ranks == 2 else sent


def others_sum(values, ranks):
    if ranks == 2:
        return swap(values)
    own = values.astype(F32)
    return (lax.psum(own, "tensor") - own).astype(BF16)


def own_rows(halves, ranks, me, rows):
    if ranks == 2:
        return jnp.where(me == 0, halves[0], halves[1])
    return lax.dynamic_slice_in_dim(jnp.concatenate(halves, axis=0), me * rows, rows)


def sum_over_all(values, devices):
    if devices & (devices - 1):
        return lax.psum(values, ("dp", "tensor"))
    step = 1
    while step < devices:
        pairs = [(device, device ^ step) for device in range(devices)]
        values = values + lax.ppermute(values, ("dp", "tensor"), pairs)
        step *= 2
    return values


def after(values, *events):
    return lax.optimization_barrier((values, *events))[0]


def on_device(
    layer_input,
    attention_norm,
    query_weight,
    key_matrix,
    value_matrix,
    query_norm,
    key_norm,
    output_weight,
    feedforward_norm,
    gate_weight,
    up_weight,
    down_weight,
    out_grad,
):
    ranks = lax.axis_size("tensor")
    me = lax.axis_index("tensor")
    depth = query_weight.shape[0]
    tok_rows, width = layer_input.shape
    groups = key_matrix.shape[1] // HEAD_SIZE
    heads = query_weight.shape[1]
    hidden = gate_weight.shape[1]

    own_attention = jnp.concatenate(
        [
            jnp.concatenate(
                [
                    query_weight.reshape(depth, groups, 2 * HEAD_SIZE),
                    key_matrix.reshape(depth, groups, HEAD_SIZE),
                    value_matrix.reshape(depth, groups, HEAD_SIZE),
                ],
                axis=2,
            ).reshape(depth, groups * GROUP),
            output_weight.T,
        ],
        axis=1,
    )
    attention_w = lax.all_gather(own_attention, "dp", axis=0, tiled=True)
    x_all = all_tokens(layer_input, send_tokens(layer_input, ranks), ranks)
    own_middle = jnp.concatenate([gate_weight, up_weight, down_weight.T], axis=1)
    middle_w = lax.all_gather(own_middle, "dp", axis=0, tiled=True)
    grad_sent = send_tokens(after(out_grad, x_all), ranks)

    cosine, sine = rope_tables()
    norm_q, norm_k = query_norm[None, :], key_norm[None, :]
    norm_two = feedforward_norm[None, :]
    input_flip, raw, rot = project(
        x_all, attention_norm[None, :], attention_w, norm_q, norm_k, cosine, sine
    )
    mixed, logs, owns, others = [], [], [], []
    for half in range(2):
        out, log = attend(after(rot, *owns), half)
        mixed.append(out)
        logs.append(log)
        owns.append(out_project(out, attention_w))
        others.append(others_sum(after(owns[half], *others), ranks))

    grad_all = all_tokens(after(out_grad, owns[0]), grad_sent, ranks)

    downs, flips, ys, f_grads, f_others = [], [], [], [], []
    for half in range(2):
        down, flip, y, f_grad = middle(
            half, after(x_all, *downs), owns[half], others[half], grad_all, norm_two, middle_w
        )
        downs.append(down)
        flips.append(flip)
        ys.append(y)
        f_grads.append(f_grad)
        if half == 0:
            f_others.append(others_sum(f_grad, ranks))
    down_part = middle_weights(flips, ys, True)
    f_others.append(others_sum(after(f_grads[1], f_others[0], down_part), ranks))
    middle_part = middle_weights(flips, ys, False, down_part)
    middle_sum = lax.psum_scatter(middle_part, "dp", scatter_dimension=0, tiled=True)
    middle_grad = middle_sum.astype(F32)

    f_others[1] = after(f_others[1], middle_part)

    residual_grads, projs, mixed_grads, norm_two_part = [], [], [], 0.0
    for half in range(2):
        residual_grad, proj, mixed_grad, part = residual_back(
            half, after(x_all, *projs), owns[half], others[half], grad_all, f_grads[half], f_others[half],
            norm_two, attention_w, heads,
        )
        residual_grads.append(residual_grad)
        projs.append(proj)
        mixed_grads.append(mixed_grad)
        norm_two_part = norm_two_part + jnp.sum(part, axis=0) / ranks

    bits, query_part, key_part = attend_back(
        rot, raw, mixed_grads, mixed, logs, norm_q, norm_k, cosine, sine
    )

    if ranks == 2:
        send = after(jnp.where(me == 0, downs[1], downs[0]), mixed_grads[1])
        down_other = swap(send)
        bits = after(bits, down_other)
        down_sum = own_rows(downs, ranks, me, tok_rows).astype(F32) + down_other.astype(F32)
    else:
        down_sum = lax.psum_scatter(
            jnp.concatenate(downs, axis=0).astype(F32), "tensor", scatter_dimension=0, tiled=True
        )
    x = layer_input.astype(F32)
    residual = x + (
        own_rows(owns, ranks, me, tok_rows).astype(F32)
        + own_rows(others, ranks, me, tok_rows).astype(F32)
    )
    layer_output = (residual + down_sum).astype(BF16)

    bits = after(bits, middle_sum)
    attention_part, sums = attention_weights(input_flip, projs, bits, mixed, attention_w)
    attention_grad = lax.psum_scatter(
        attention_part, "dp", scatter_dimension=0, tiled=True
    ).astype(F32)
    norm_one_part = jnp.sum(sums, axis=1) / attention_norm
    if ranks == 2:
        other = swap(input_back(1 - me, tok_rows, bits, attention_w))
        own = input_back(me, tok_rows, bits, attention_w)
        attention_input_grad = own.astype(F32) + other.astype(F32)
    else:
        attention_input_grad = lax.psum_scatter(
            input_back(jnp.zeros_like(me), SEQ_LEN, bits, attention_w).astype(F32),
            "tensor",
            scatter_dimension=0,
            tiled=True,
        )
    scale = lax.rsqrt(jnp.mean(x * x, axis=-1, keepdims=True) + epsilon)
    normed = x * scale
    u = attention_input_grad * attention_norm
    input_grad = own_rows(residual_grads, ranks, me, tok_rows) + scale * (
        u - normed * jnp.mean(u * normed, axis=-1, keepdims=True)
    )
    sums = sum_over_all(
        jnp.concatenate(
            [
                norm_one_part,
                norm_two_part,
                jnp.sum(query_part, axis=(0, 1)),
                jnp.sum(key_part, axis=(0, 1)),
            ]
        ).reshape(-1, HEAD_SIZE),
        lax.axis_size("dp") * ranks,
    ).reshape(-1)
    attention_norm_grad, feedforward_norm_grad, query_norm_grad, key_norm_grad = jnp.split(
        sums, [width, 2 * width, 2 * width + HEAD_SIZE]
    )
    qkv_grad = attention_grad[:, : groups * GROUP].reshape(depth, groups, GROUP)
    return (
        layer_output,
        input_grad,
        attention_norm_grad,
        qkv_grad[:, :, : 2 * HEAD_SIZE].reshape(depth, -1),
        qkv_grad[:, :, 2 * HEAD_SIZE : 3 * HEAD_SIZE].reshape(depth, -1),
        qkv_grad[:, :, 3 * HEAD_SIZE :].reshape(depth, -1),
        query_norm_grad,
        key_norm_grad,
        attention_grad[:, groups * GROUP :].T,
        feedforward_norm_grad,
        middle_grad[:, :hidden],
        middle_grad[:, hidden : 2 * hidden],
        middle_grad[:, 2 * hidden :].T,
    )


def solution(mesh):
    return jax.shard_map(
        on_device,
        mesh=mesh,
        in_specs=(
            P(("dp", "tensor"), None),
            P(),
            P("dp", "tensor"),
            P("dp", "tensor"),
            P("dp", "tensor"),
            P(),
            P(),
            P("tensor", "dp"),
            P(),
            P("dp", "tensor"),
            P("dp", "tensor"),
            P("tensor", "dp"),
            P(("dp", "tensor"), None),
        ),
        out_specs=(
            P(("dp", "tensor"), None),
            P(("dp", "tensor"), None),
            P(),
            P("dp", "tensor"),
            P("dp", "tensor"),
            P("dp", "tensor"),
            P(),
            P(),
            P("tensor", "dp"),
            P(),
            P("dp", "tensor"),
            P("dp", "tensor"),
            P("tensor", "dp"),
        ),
        check_vma=False,
    )
```

```python
import math

import jax
import jax.numpy as jnp
from jax import lax
from jax.experimental import pallas as pl
from jax.experimental.pallas import tpu as pltpu
from jax.sharding import PartitionSpec as P

HEAD_SIZE = 128
SEQ_LEN = 2048

epsilon = 1e-06
rope_base = 1000000.0
masked_score = -1e30
LN2 = math.log(2.0)
SCORE_SCALE = HEAD_SIZE ** (-0.5)
GROUP = 4 * HEAD_SIZE
F32 = jnp.float32
BF16 = jnp.bfloat16
VMEM_LIMIT = 60 * 1024 * 1024
HALF = SEQ_LEN // 2


def nn(left, right):
    return lax.dot_general(left, right, (((1,), (0,)), ((), ())), preferred_element_type=F32)


def nt(left, right):
    return lax.dot_general(left, right, (((1,), (1,)), ((), ())), preferred_element_type=F32)


def row_mean(values):
    ones = jnp.full((HEAD_SIZE, HEAD_SIZE), 1.0 / HEAD_SIZE, BF16)
    return nn(values.astype(BF16), ones)


def rope_tables():
    position = jnp.arange(SEQ_LEN).astype(F32)
    inverse = jnp.power(rope_base, -jnp.arange(HEAD_SIZE // 2).astype(F32) * (2.0 / HEAD_SIZE))
    angles = position[:, None] * inverse[None, :]
    cosine, sine = jnp.cos(angles), jnp.sin(angles)
    return (
        jnp.concatenate([cosine, cosine], axis=1),
        jnp.concatenate([-sine, sine], axis=1),
    )


def params(*semantics):
    return pltpu.CompilerParams(dimension_semantics=semantics, vmem_limit_bytes=VMEM_LIMIT)


def cost(flops, rate):
    return pl.CostEstimate(flops=int(flops * (1000.0 / rate)), bytes_accessed=0, transcendentals=0)


def whole(shape):
    return pl.BlockSpec(shape, lambda *_: (0,) * len(shape), pipeline_mode=pl.Buffered(1))


def out_weight_spec(width, heads):
    return pl.BlockSpec((width, heads), lambda *_: (0, 2), pipeline_mode=pl.Buffered(1))


def project_kernel(x_ref, gain_ref, w_ref, qn_ref, kn_ref, cos_ref, sin_ref, at_ref, raw_ref, rot_ref):
    x = x_ref[...].astype(F32)
    scale = lax.rsqrt(jnp.mean(x * x, axis=-1, keepdims=True) + epsilon)
    a = (x * scale * gain_ref[...]).astype(BF16)
    at_ref[...] = a.T
    cosine, sine = cos_ref[...], sin_ref[...]
    for group in range(w_ref.shape[1] // GROUP):
        base = group * GROUP
        y = nn(a, w_ref[:, base : base + GROUP])
        raw_ref[:, base : base + GROUP] = y.astype(BF16)
        for head in range(3):
            z = y[:, head * HEAD_SIZE : (head + 1) * HEAD_SIZE]
            gain = kn_ref[...] * (SCORE_SCALE / LN2) if head == 2 else qn_ref[...]
            z = z * lax.rsqrt(jnp.mean(z * z, axis=-1, keepdims=True) + epsilon) * gain
            z = z * cosine + pltpu.roll(z, HEAD_SIZE // 2, 1) * sine
            rot_ref[:, base + head * HEAD_SIZE : base + (head + 1) * HEAD_SIZE] = z.astype(BF16)
        rot_ref[:, base + 3 * HEAD_SIZE : base + GROUP] = y[:, 3 * HEAD_SIZE :].astype(BF16)


def project(x, gain, weights, query_norm, key_norm, cosine, sine):
    tokens, width = x.shape
    columns = weights.shape[1] // 3 * 2
    rows = 256
    return pl.pallas_call(
        project_kernel,
        grid=(tokens // rows,),
        in_specs=[
            pl.BlockSpec((rows, width), lambda i: (i, 0)),
            whole((1, width)),
            whole((width, columns)),
            whole((1, HEAD_SIZE)),
            whole((1, HEAD_SIZE)),
            pl.BlockSpec((rows, HEAD_SIZE), lambda i: (i, 0)),
            pl.BlockSpec((rows, HEAD_SIZE), lambda i: (i, 0)),
        ],
        out_specs=[
            pl.BlockSpec((width, rows), lambda i: (0, i)),
            pl.BlockSpec((rows, columns), lambda i: (i, 0)),
            pl.BlockSpec((rows, columns), lambda i: (i, 0)),
        ],
        out_shape=[
            jax.ShapeDtypeStruct((width, tokens), BF16),
            jax.ShapeDtypeStruct((tokens, columns), BF16),
            jax.ShapeDtypeStruct((tokens, columns), BF16),
        ],
        compiler_params=params("arbitrary"),
        cost_estimate=cost(2 * tokens * width * columns, 500),
        name="project",
    )(x, gain, weights, query_norm, key_norm, cosine, sine)


BLOCK = 512


def split_three(values):
    lane = lax.broadcasted_iota(jnp.int32, values.shape, 1)
    high = values.astype(BF16).astype(F32)
    rest = values - high
    middle = rest.astype(BF16).astype(F32)
    low = rest - middle
    return jnp.where(
        lane == 0, high, jnp.where(lane == 1, middle, jnp.where(lane == 2, low, 0.0))
    ).astype(BF16)


def attend_kernel(first, q_ref, k_ref, v_ref, out_ref, log_ref, v_ones, acc):
    i = pl.program_id(1)

    @pl.when(i == 0)
    def _():
        v_ones[:, :HEAD_SIZE] = v_ref[...]
        v_ones[:, HEAD_SIZE:] = jnp.ones(v_ref.shape, BF16)

    acc[...] = jnp.zeros_like(acc)

    def tile(row, rows, start, size, masked):
        keys = k_ref[pl.ds(start, size), :]
        values = v_ones[pl.ds(start, size), :]
        for head in range(2):
            s = nt(q_ref[row : row + rows, head * HEAD_SIZE : (head + 1) * HEAD_SIZE], keys)
            if masked:
                query = lax.broadcasted_iota(jnp.int32, s.shape, 0)
                key = lax.broadcasted_iota(jnp.int32, s.shape, 1)
                s = jnp.where(key <= query + (size - rows), s, masked_score)
            acc[head, row : row + rows] += nn(jnp.exp2(s).astype(BF16), values)

    def step(j, carry):
        tile(0, BLOCK, pl.multiple_of(j * BLOCK, BLOCK), BLOCK, False)
        return carry

    lax.fori_loop(0, i + first, step, 0)
    start = pl.multiple_of((i + first) * BLOCK, BLOCK)
    tile(0, BLOCK // 2, start, BLOCK // 2, True)
    tile(BLOCK // 2, BLOCK // 2, start, BLOCK, True)
    for head in range(2):
        columns = slice(head * HEAD_SIZE, (head + 1) * HEAD_SIZE)
        total = acc[head, :, HEAD_SIZE:]
        out_ref[:, columns] = (acc[head, :, :HEAD_SIZE] / total).astype(BF16)
        log_ref[:, columns] = split_three(jnp.log(total) * (-1.0 / LN2))


def attend(rot, half):
    groups = rot.shape[1] // GROUP
    width = 2 * HEAD_SIZE
    blocks = HALF // BLOCK
    first = half * blocks
    keys = HALF * (half + 1)
    return pl.pallas_call(
        lambda *refs: attend_kernel(first, *refs),
        grid=(groups, blocks),
        in_specs=[
            pl.BlockSpec((BLOCK, width), lambda c, i: (i + first, 2 * c)),
            pl.BlockSpec((keys, HEAD_SIZE), lambda c, i: (0, 4 * c + 2)),
            pl.BlockSpec((keys, HEAD_SIZE), lambda c, i: (0, 4 * c + 3)),
        ],
        out_specs=[
            pl.BlockSpec((BLOCK, width), lambda c, i: (i, c)),
            pl.BlockSpec((BLOCK, width), lambda c, i: (i, c)),
        ],
        out_shape=[
            jax.ShapeDtypeStruct((HALF, groups * width), BF16),
            jax.ShapeDtypeStruct((HALF, groups * width), BF16),
        ],
        scratch_shapes=[
            pltpu.VMEM((keys, width), BF16),
            pltpu.VMEM((2, BLOCK, width), F32),
        ],
        compiler_params=params("arbitrary", "arbitrary"),
        cost_estimate=cost(4 * HALF * keys * groups * width, 500),
        name="attend",
    )(rot, rot, rot)


def out_project_kernel(mixed_ref, w_ref, out_ref):
    out_ref[...] = nt(mixed_ref[...], w_ref[...]).astype(BF16)


def out_project(mixed, weights):
    rows = 256
    width, heads = weights.shape[0], mixed.shape[1]
    return pl.pallas_call(
        out_project_kernel,
        grid=(HALF // rows,),
        in_specs=[
            pl.BlockSpec((rows, heads), lambda i: (i, 0)),
            out_weight_spec(width, heads),
        ],
        out_specs=pl.BlockSpec((rows, width), lambda i: (i, 0)),
        out_shape=jax.ShapeDtypeStruct((HALF, width), BF16),
        compiler_params=params("arbitrary"),
        cost_estimate=cost(2 * HALF * width * heads, 350),
        name="out_project",
    )(mixed, weights)


ROWS = 256


def attend_back_kernel(
    rot_ref, raw_ref, do_a, do_b, out_a, out_b, log_a, log_b, qn_ref, kn_ref, cos_ref, sin_ref,
    bits_ref, qg_ref, kg_ref,
    grads, log_row, delta_row, k_flip, dq_flip, dk, dv,
):
    blocks = SEQ_LEN // BLOCK
    ones = jnp.ones((8, HEAD_SIZE), BF16)

    def prepare(half, do_ref, out_ref, log_ref):
        def body(r, carry):
            near = pl.ds(pl.multiple_of(r * ROWS, ROWS), ROWS)
            rows = pl.ds(pl.multiple_of(half * HALF + r * ROWS, ROWS), ROWS)
            k_flip[:, rows] = rot_ref[rows, 2 * HEAD_SIZE : 3 * HEAD_SIZE].T
            grad = do_ref[near, :]
            grads[rows, :] = grad
            product = grad.astype(F32) * out_ref[near, :].astype(F32)
            high = product.astype(BF16)
            low = (product - high.astype(F32)).astype(BF16)
            for head in range(2):
                columns = slice(head * HEAD_SIZE, (head + 1) * HEAD_SIZE)
                log_row[head, :, rows] = nt(ones, log_ref[near, columns])
                delta_row[head, :, rows] = nt(ones, high[:, columns]) + nt(ones, low[:, columns])
            return carry

        lax.fori_loop(0, HALF // ROWS, body, 0)

    prepare(0, do_a, out_a, log_a)
    prepare(1, do_b, out_b, log_b)
    dq_flip[...] = jnp.zeros_like(dq_flip)

    def tile(kv_start, kv_size, start, size, masked):
        kv, q_rows = pl.ds(kv_start, kv_size), pl.ds(start, size)
        keys = rot_ref[kv, 2 * HEAD_SIZE : 3 * HEAD_SIZE]
        values = rot_ref[kv, 3 * HEAD_SIZE :]
        for head in range(2):
            columns = slice(head * HEAD_SIZE, (head + 1) * HEAD_SIZE)
            q = rot_ref[q_rows, columns]
            d = grads[q_rows, columns]
            s = nt(keys, q) + log_row[head, :1, q_rows]
            if masked:
                row = lax.broadcasted_iota(jnp.int32, s.shape, 0)
                column = lax.broadcasted_iota(jnp.int32, s.shape, 1)
                s = jnp.where(row <= column, s, masked_score)
            p = jnp.exp2(s)
            ds = (p * (nt(values, d) - delta_row[head, :1, q_rows])).astype(BF16)
            new_dv = nn(p.astype(BF16), d)
            new_dk = nn(ds, q)
            if masked and head == 0:
                dv[kv, :] = new_dv
                dk[kv, :] = new_dk
            else:
                dv[kv, :] += new_dv
                dk[kv, :] += new_dk
            dq_flip[head, :, q_rows] += nn(k_flip[:, kv], ds)

    part = BLOCK // 2

    def key_block(j, carry):
        start = pl.multiple_of(j * BLOCK, BLOCK)
        later = pl.multiple_of(j * BLOCK + part, part)
        tile(start, part, start, BLOCK, True)
        tile(later, part, later, part, True)

        def query_block(i, inner):
            tile(start, BLOCK, pl.multiple_of(i * BLOCK, BLOCK), BLOCK, False)
            return inner

        return lax.fori_loop(j + 1, blocks, query_block, carry)

    lax.fori_loop(0, blocks, key_block, 0)

    qg_ref[...] = jnp.zeros_like(qg_ref)
    kg_ref[...] = jnp.zeros_like(kg_ref)

    def finish(r, carry):
        rows = pl.ds(pl.multiple_of(r * ROWS, ROWS), ROWS)
        cosine, sine = cos_ref[rows, :], sin_ref[rows, :]
        for head in range(3):
            columns = slice(head * HEAD_SIZE, (head + 1) * HEAD_SIZE)
            if head < 2:
                u = dq_flip[head, :, rows].T * LN2
                gain, total = qn_ref[...], qg_ref
            else:
                u = dk[rows, :] * SCORE_SCALE
                gain, total = kn_ref[...], kg_ref
            u = u * cosine - pltpu.roll(u, HEAD_SIZE // 2, 1) * sine
            x = raw_ref[rows, columns].astype(F32)
            scale = lax.rsqrt(row_mean(x * x) + epsilon)
            x = x * scale
            total[0] += jnp.sum((u * x).reshape(ROWS // 8, 8, HEAD_SIZE), axis=0)
            w = u * gain
            bits_ref[rows, columns] = (
                scale * (w - x * row_mean(w * x))
            ).astype(BF16)
        bits_ref[rows, 3 * HEAD_SIZE :] = dv[rows, :].astype(BF16)
        return carry

    lax.fori_loop(0, SEQ_LEN // ROWS, finish, 0)


def attend_back(rot, raw, grads, outs, logs, query_norm, key_norm, cosine, sine):
    groups = rot.shape[1] // GROUP
    width = 2 * HEAD_SIZE
    return pl.pallas_call(
        attend_back_kernel,
        grid=(groups,),
        in_specs=[
            pl.BlockSpec((SEQ_LEN, GROUP), lambda c: (0, c)),
            pl.BlockSpec((SEQ_LEN, GROUP), lambda c: (0, c)),
            *[pl.BlockSpec((HALF, width), lambda c: (0, c))] * 6,
            whole((1, HEAD_SIZE)),
            whole((1, HEAD_SIZE)),
            whole((SEQ_LEN, HEAD_SIZE)),
            whole((SEQ_LEN, HEAD_SIZE)),
        ],
        out_specs=[
            pl.BlockSpec((SEQ_LEN, GROUP), lambda c: (0, c)),
            pl.BlockSpec((1, 8, HEAD_SIZE), lambda c: (c, 0, 0)),
            pl.BlockSpec((1, 8, HEAD_SIZE), lambda c: (c, 0, 0)),
        ],
        out_shape=[
            jax.ShapeDtypeStruct((SEQ_LEN, groups * GROUP), BF16),
            jax.ShapeDtypeStruct((groups, 8, HEAD_SIZE), F32),
            jax.ShapeDtypeStruct((groups, 8, HEAD_SIZE), F32),
        ],
        scratch_shapes=[
            pltpu.VMEM((SEQ_LEN, width), BF16),
            pltpu.VMEM((2, 8, SEQ_LEN), F32),
            pltpu.VMEM((2, 8, SEQ_LEN), F32),
            pltpu.VMEM((HEAD_SIZE, SEQ_LEN), BF16),
            pltpu.VMEM((2, HEAD_SIZE, SEQ_LEN), F32),
            pltpu.VMEM((SEQ_LEN, HEAD_SIZE), F32),
            pltpu.VMEM((SEQ_LEN, HEAD_SIZE), F32),
        ],
        compiler_params=params("arbitrary"),
        cost_estimate=cost(5 * SEQ_LEN * SEQ_LEN * groups * width, 80),
        name="attend_back",
    )(rot, raw, *grads, *outs, *logs, query_norm, key_norm, cosine, sine)


def residual_of(x_ref, own_ref, other_ref):
    residual = x_ref[...].astype(F32) + (own_ref[...].astype(F32) + other_ref[...].astype(F32))
    scale = lax.rsqrt(jnp.mean(residual * residual, axis=-1, keepdims=True) + epsilon)
    return residual * scale, scale


def middle_kernel(
    x_ref, own_ref, other_ref, grad_ref, fn_ref, w_ref, down_ref, flip_ref, y_ref, fg_ref
):
    width, columns = w_ref.shape
    hidden = columns // 3
    chunk = 512 if hidden % 512 == 0 else hidden
    rows = x_ref.shape[0]
    normed, scale = residual_of(x_ref, own_ref, other_ref)
    f = (normed * fn_ref[...]).astype(BF16)
    grad = grad_ref[...]
    flip_ref[0] = f.T
    flip_ref[1] = grad.T
    total = jnp.zeros((rows, width), F32)
    f_grad = jnp.zeros((rows, width), F32)
    for start in range(0, hidden, chunk):
        gate_w = w_ref[:, start : start + chunk]
        up_w = w_ref[:, hidden + start : hidden + start + chunk]
        down_w = w_ref[:, 2 * hidden + start : 2 * hidden + start + chunk]
        gate, up = nn(f, gate_w), nn(f, up_w)
        sig = 1.0 / (1.0 + jnp.exp(-gate))
        silu = gate * sig
        low = (silu * up).astype(BF16)
        total += nt(low, down_w)
        hidden_grad = nn(grad, down_w)
        gate_bits = (hidden_grad * up * (sig * (1.0 + gate * (1.0 - sig)))).astype(BF16)
        up_bits = (hidden_grad * silu).astype(BF16)
        y_ref[:, start : start + chunk] = gate_bits
        y_ref[:, hidden + start : hidden + start + chunk] = up_bits
        y_ref[:, 2 * hidden + start : 2 * hidden + start + chunk] = low
        f_grad += nt(gate_bits, gate_w) + nt(up_bits, up_w)
    down_ref[...] = total.astype(BF16)
    fg_ref[...] = f_grad.astype(BF16)


def half_rows(rows, width, half):
    return pl.BlockSpec((rows, width), lambda i: (i + half * (HALF // rows), 0))


def middle(half, x_all, own, other, grad_all, gain, weights):
    width, columns = weights.shape
    rows = 256
    near = pl.BlockSpec((rows, width), lambda i: (i, 0))
    return pl.pallas_call(
        middle_kernel,
        grid=(HALF // rows,),
        in_specs=[
            half_rows(rows, width, half), near, near, half_rows(rows, width, half),
            whole((1, width)), whole(weights.shape),
        ],
        out_specs=[
            near,
            pl.BlockSpec((2, width, rows), lambda i: (0, 0, i)),
            pl.BlockSpec((rows, columns), lambda i: (i, 0)),
            near,
        ],
        out_shape=[
            jax.ShapeDtypeStruct((HALF, width), BF16),
            jax.ShapeDtypeStruct((2, width, HALF), BF16),
            jax.ShapeDtypeStruct((HALF, columns), BF16),
            jax.ShapeDtypeStruct((HALF, width), BF16),
        ],
        compiler_params=params("arbitrary"),
        cost_estimate=cost(4 * HALF * width * columns, 2500),
        name="middle",
    )(x_all, own, other, grad_all, gain, weights)


def residual_back_kernel(
    x_ref, own_ref, other_ref, grad_ref, fg_ref, fg_other_ref, fn_ref, w_ref,
    rg_ref, flip_ref, mg_ref, fng_ref,
):
    rows, width = x_ref.shape
    normed, scale = residual_of(x_ref, own_ref, other_ref)
    f_grad = fg_ref[...].astype(F32) + fg_other_ref[...].astype(F32)

    @pl.when(pl.program_id(0) == 0)
    def _():
        fng_ref[...] = jnp.zeros_like(fng_ref)

    fng_ref[...] += jnp.sum((f_grad * normed).reshape(rows // 8, 8, width), axis=0)
    u = f_grad * fn_ref[...]
    residual_grad = grad_ref[...].astype(F32) + scale * (
        u - normed * jnp.mean(u * normed, axis=-1, keepdims=True)
    )
    rg_ref[...] = residual_grad
    proj = residual_grad.astype(BF16)
    flip_ref[...] = proj.T
    mg_ref[...] = nn(proj, w_ref[...]).astype(BF16)


def residual_back(half, x_all, own, other, grad_all, fg, fg_other, gain, weights, heads):
    width = weights.shape[0]
    rows = 256
    near = pl.BlockSpec((rows, width), lambda i: (i, 0))
    return pl.pallas_call(
        residual_back_kernel,
        grid=(HALF // rows,),
        in_specs=[
            half_rows(rows, width, half), near, near, half_rows(rows, width, half), near, near,
            whole((1, width)), out_weight_spec(width, heads),
        ],
        out_specs=[
            near,
            pl.BlockSpec((width, rows), lambda i: (0, i)),
            pl.BlockSpec((rows, heads), lambda i: (i, 0)),
            pl.BlockSpec((8, width), lambda i: (0, 0)),
        ],
        out_shape=[
            jax.ShapeDtypeStruct((HALF, width), F32),
            jax.ShapeDtypeStruct((width, HALF), BF16),
            jax.ShapeDtypeStruct((HALF, heads), BF16),
            jax.ShapeDtypeStruct((8, width), F32),
        ],
        compiler_params=params("arbitrary"),
        cost_estimate=cost(2 * HALF * width * heads, 190),
        name="residual_back",
    )(x_all, own, other, grad_all, fg, fg_other, gain, weights)


def middle_weights_kernel(which, flip_a, flip_b, y_a, y_b, *rest):
    rest[-1][...] = (nn(flip_a[which], y_a[...]) + nn(flip_b[which], y_b[...])).astype(BF16)


def middle_weights(flips, ys, down, *partial):
    width = flips[0].shape[1]
    columns = ys[0].shape[1]
    hidden = columns // 3
    size = 512 if hidden % 512 == 0 else hidden
    bound = 2 * hidden // size
    first, blocks = (bound, columns // size - bound) if down else (0, bound)
    which = 1 if down else 0
    spec = pl.BlockSpec((HALF, size), lambda i: (0, i + first))
    flip_spec = pl.BlockSpec(
        (1, width, HALF), lambda i: (which, 0, 0), pipeline_mode=pl.Buffered(1)
    )
    return pl.pallas_call(
        lambda *refs: middle_weights_kernel(0, *refs),
        grid=(blocks,),
        in_specs=[flip_spec, flip_spec, spec, spec] + [pl.BlockSpec(memory_space=pl.ANY)] * len(partial),
        out_specs=pl.BlockSpec((width, size), lambda i: (0, i + first)),
        out_shape=jax.ShapeDtypeStruct((width, columns), BF16),
        input_output_aliases={4: 0} if partial else {},
        compiler_params=params("arbitrary"),
        cost_estimate=cost(2 * SEQ_LEN * width * size * blocks, 3000),
        name="down_weights" if down else "gate_up_weights",
    )(*flips, *ys, *partial)


def attention_weights_kernel(
    bound, input_flip, proj_a, proj_b, bits_ref, mixed_a, mixed_b, w_ref, out_ref, sums_ref
):
    i = pl.program_id(0)

    @pl.when(i == 0)
    def _():
        sums_ref[...] = jnp.zeros_like(sums_ref)

    @pl.when(i < bound)
    def _():
        out = nn(input_flip[...], bits_ref[...])
        out_ref[...] = out.astype(BF16)
        product = out * w_ref[...].astype(F32)
        for start in range(0, product.shape[1], 128):
            sums_ref[...] += product[:, start : start + 128]

    @pl.when(i >= bound)
    def _():
        out_ref[...] = (nn(proj_a[...], mixed_a[...]) + nn(proj_b[...], mixed_b[...])).astype(BF16)


def attention_weights(input_flip, projs, bits, mixed, weights):
    width, columns = weights.shape
    heads = columns // 3
    size = math.gcd(512, heads)
    bound = 2 * heads // size
    mixed_spec = pl.BlockSpec((HALF, size), lambda i: (0, jnp.maximum(i - bound, 0)))
    return pl.pallas_call(
        lambda *refs: attention_weights_kernel(bound, *refs),
        grid=(columns // size,),
        in_specs=[
            whole(input_flip.shape), whole(projs[0].shape), whole(projs[1].shape),
            pl.BlockSpec((SEQ_LEN, size), lambda i: (0, jnp.minimum(i, bound - 1))),
            mixed_spec, mixed_spec,
            pl.BlockSpec((width, size), lambda i: (0, i)),
        ],
        out_specs=[
            pl.BlockSpec((width, size), lambda i: (0, i)),
            pl.BlockSpec((width, 128), lambda i: (0, 0)),
        ],
        out_shape=[
            jax.ShapeDtypeStruct((width, columns), BF16),
            jax.ShapeDtypeStruct((width, 128), F32),
        ],
        compiler_params=params("arbitrary"),
        cost_estimate=cost(2 * SEQ_LEN * width * columns, 640),
        name="attention_weights",
    )(input_flip, *projs, bits, *mixed, weights)


def input_back_kernel(place_ref, bits_ref, w_ref, out_ref):
    out_ref[...] = nt(bits_ref[...], w_ref[...]).astype(BF16)


def input_back(place, tokens, bits, weights):
    width = weights.shape[0]
    columns = bits.shape[1]
    rows = 256
    blocks = tokens // rows
    return pl.pallas_call(
        input_back_kernel,
        grid_spec=pltpu.PrefetchScalarGridSpec(
            num_scalar_prefetch=1,
            grid=(blocks,),
            in_specs=[
                pl.BlockSpec((rows, columns), lambda i, place: (place[0] * blocks + i, 0)),
                whole((width, columns)),
            ],
            out_specs=pl.BlockSpec((rows, width), lambda i, place: (i, 0)),
        ),
        out_shape=jax.ShapeDtypeStruct((tokens, width), BF16),
        compiler_params=params("arbitrary"),
        cost_estimate=cost(2 * tokens * width * columns, 480),
        name="input_back",
    )(place.reshape(1), bits, weights)


def swap(values):
    return lax.ppermute(values, "tensor", [(0, 1), (1, 0)])


def in_order(own, other, axis):
    first = lax.axis_index("tensor") == 0
    return jnp.concatenate(
        [jnp.where(first, own, other), jnp.where(first, other, own)], axis=axis
    )


def send_tokens(values, ranks):
    if ranks == 2:
        return swap(values)
    return lax.all_gather(values, "tensor", axis=0, tiled=True)


def all_tokens(own, sent, ranks):
    return in_order(own, sent, 0) if ranks == 2 else sent


def others_sum(values, ranks):
    if ranks == 2:
        return swap(values)
    own = values.astype(F32)
    return (lax.psum(own, "tensor") - own).astype(BF16)


def own_rows(halves, ranks, me, rows):
    if ranks == 2:
        return jnp.where(me == 0, halves[0], halves[1])
    return lax.dynamic_slice_in_dim(jnp.concatenate(halves, axis=0), me * rows, rows)


def sum_over_all(values, devices):
    if devices & (devices - 1):
        return lax.psum(values, ("dp", "tensor"))
    step = 1
    while step < devices:
        pairs = [(device, device ^ step) for device in range(devices)]
        values = values + lax.ppermute(values, ("dp", "tensor"), pairs)
        step *= 2
    return values


def after(values, *events):
    return lax.optimization_barrier((values, *events))[0]


def on_device(
    layer_input,
    attention_norm,
    query_weight,
    key_matrix,
    value_matrix,
    query_norm,
    key_norm,
    output_weight,
    feedforward_norm,
    gate_weight,
    up_weight,
    down_weight,
    out_grad,
):
    ranks = lax.axis_size("tensor")
    me = lax.axis_index("tensor")
    depth = query_weight.shape[0]
    tok_rows, width = layer_input.shape
    groups = key_matrix.shape[1] // HEAD_SIZE
    heads = query_weight.shape[1]
    hidden = gate_weight.shape[1]

    own_attention = jnp.concatenate(
        [
            jnp.concatenate(
                [
                    query_weight.reshape(depth, groups, 2 * HEAD_SIZE),
                    key_matrix.reshape(depth, groups, HEAD_SIZE),
                    value_matrix.reshape(depth, groups, HEAD_SIZE),
                ],
                axis=2,
            ).reshape(depth, groups * GROUP),
            output_weight.T,
        ],
        axis=1,
    )
    attention_w = lax.all_gather(own_attention, "dp", axis=0, tiled=True)
    x_all = all_tokens(layer_input, send_tokens(layer_input, ranks), ranks)
    own_middle = jnp.concatenate([gate_weight, up_weight, down_weight.T], axis=1)
    middle_w = lax.all_gather(own_middle, "dp", axis=0, tiled=True)
    grad_sent = send_tokens(after(out_grad, x_all), ranks)

    cosine, sine = rope_tables()
    norm_q, norm_k = query_norm[None, :], key_norm[None, :]
    norm_two = feedforward_norm[None, :]
    input_flip, raw, rot = project(
        x_all, attention_norm[None, :], attention_w, norm_q, norm_k, cosine, sine
    )
    mixed, logs, owns, others = [], [], [], []
    for half in range(2):
        out, log = attend(after(rot, *owns), half)
        mixed.append(out)
        logs.append(log)
        owns.append(out_project(out, attention_w))
        others.append(others_sum(after(owns[half], *others), ranks))

    grad_all = all_tokens(after(out_grad, owns[0]), grad_sent, ranks)

    downs, flips, ys, f_grads, f_others = [], [], [], [], []
    for half in range(2):
        down, flip, y, f_grad = middle(
            half, after(x_all, *downs), owns[half], others[half], grad_all, norm_two, middle_w
        )
        downs.append(down)
        flips.append(flip)
        ys.append(y)
        f_grads.append(f_grad)
        if half == 0:
            f_others.append(others_sum(f_grad, ranks))
    down_part = middle_weights(flips, ys, True)
    f_others.append(others_sum(after(f_grads[1], f_others[0], down_part), ranks))
    middle_part = middle_weights(flips, ys, False, down_part)
    middle_sum = lax.psum_scatter(middle_part, "dp", scatter_dimension=0, tiled=True)
    middle_grad = middle_sum.astype(F32)

    f_others[1] = after(f_others[1], middle_part)

    residual_grads, projs, mixed_grads, norm_two_part = [], [], [], 0.0
    for half in range(2):
        residual_grad, proj, mixed_grad, part = residual_back(
            half, after(x_all, *projs), owns[half], others[half], grad_all, f_grads[half], f_others[half],
            norm_two, attention_w, heads,
        )
        residual_grads.append(residual_grad)
        projs.append(proj)
        mixed_grads.append(mixed_grad)
        norm_two_part = norm_two_part + jnp.sum(part, axis=0) / ranks

    bits, query_part, key_part = attend_back(
        rot, raw, mixed_grads, mixed, logs, norm_q, norm_k, cosine, sine
    )

    if ranks == 2:
        send = after(jnp.where(me == 0, downs[1], downs[0]), mixed_grads[1])
        down_other = swap(send)
        bits = after(bits, down_other)
        down_sum = own_rows(downs, ranks, me, tok_rows).astype(F32) + down_other.astype(F32)
    else:
        down_sum = lax.psum_scatter(
            jnp.concatenate(downs, axis=0).astype(F32), "tensor", scatter_dimension=0, tiled=True
        )
    x = layer_input.astype(F32)
    residual = x + (
        own_rows(owns, ranks, me, tok_rows).astype(F32)
        + own_rows(others, ranks, me, tok_rows).astype(F32)
    )
    layer_output = (residual + down_sum).astype(BF16)

    bits = after(bits, middle_sum)
    attention_part, sums = attention_weights(input_flip, projs, bits, mixed, attention_w)
    attention_grad = lax.psum_scatter(
        attention_part, "dp", scatter_dimension=0, tiled=True
    ).astype(F32)
    norm_one_part = jnp.sum(sums, axis=1) / attention_norm
    if ranks == 2:
        other = swap(input_back(1 - me, tok_rows, bits, attention_w))
        own = input_back(me, tok_rows, bits, attention_w)
        attention_input_grad = own.astype(F32) + other.astype(F32)
    else:
        attention_input_grad = lax.psum_scatter(
            input_back(jnp.zeros_like(me), SEQ_LEN, bits, attention_w).astype(F32),
            "tensor",
            scatter_dimension=0,
            tiled=True,
        )
    scale = lax.rsqrt(jnp.mean(x * x, axis=-1, keepdims=True) + epsilon)
    normed = x * scale
    u = attention_input_grad * attention_norm
    input_grad = own_rows(residual_grads, ranks, me, tok_rows) + scale * (
        u - normed * jnp.mean(u * normed, axis=-1, keepdims=True)
    )
    sums = sum_over_all(
        jnp.concatenate(
            [
                norm_one_part,
                norm_two_part,
                jnp.sum(query_part, axis=(0, 1)),
                jnp.sum(key_part, axis=(0, 1)),
            ]
        ).reshape(-1, HEAD_SIZE),
        lax.axis_size("dp") * ranks,
    ).reshape(-1)
    attention_norm_grad, feedforward_norm_grad, query_norm_grad, key_norm_grad = jnp.split(
        sums, [width, 2 * width, 2 * width + HEAD_SIZE]
    )
    qkv_grad = attention_grad[:, : groups * GROUP].reshape(depth, groups, GROUP)
    return (
        layer_output,
        input_grad,
        attention_norm_grad,
        qkv_grad[:, :, : 2 * HEAD_SIZE].reshape(depth, -1),
        qkv_grad[:, :, 2 * HEAD_SIZE : 3 * HEAD_SIZE].reshape(depth, -1),
        qkv_grad[:, :, 3 * HEAD_SIZE :].reshape(depth, -1),
        query_norm_grad,
        key_norm_grad,
        attention_grad[:, groups * GROUP :].T,
        feedforward_norm_grad,
        middle_grad[:, :hidden],
        middle_grad[:, hidden : 2 * hidden],
        middle_grad[:, 2 * hidden :].T,
    )


def solution(mesh):
    return jax.shard_map(
        on_device,
        mesh=mesh,
        in_specs=(
            P(("dp", "tensor"), None),
            P(),
            P("dp", "tensor"),
            P("dp", "tensor"),
            P("dp", "tensor"),
            P(),
            P(),
            P("tensor", "dp"),
            P(),
            P("dp", "tensor"),
            P("dp", "tensor"),
            P("tensor", "dp"),
            P(("dp", "tensor"), None),
        ),
        out_specs=(
            P(("dp", "tensor"), None),
            P(("dp", "tensor"), None),
            P(),
            P("dp", "tensor"),
            P("dp", "tensor"),
            P("dp", "tensor"),
            P(),
            P(),
            P("tensor", "dp"),
            P(),
            P("dp", "tensor"),
            P("dp", "tensor"),
            P("tensor", "dp"),
        ),
        check_vma=False,
    )
```

```python
import math

import jax
import jax.numpy as jnp
from jax import lax
from jax.experimental import pallas as pl
from jax.experimental.pallas import tpu as pltpu
from jax.sharding import PartitionSpec as P

HEAD_SIZE = 128
SEQ_LEN = 2048

epsilon = 1e-06
rope_base = 1000000.0
masked_score = -1e30
LN2 = math.log(2.0)
SCORE_SCALE = HEAD_SIZE ** (-0.5)
GROUP = 4 * HEAD_SIZE
F32 = jnp.float32
BF16 = jnp.bfloat16
VMEM_LIMIT = 60 * 1024 * 1024
HALF = SEQ_LEN // 2


def nn(left, right):
    return lax.dot_general(left, right, (((1,), (0,)), ((), ())), preferred_element_type=F32)


def nt(left, right):
    return lax.dot_general(left, right, (((1,), (1,)), ((), ())), preferred_element_type=F32)


def row_mean(values):
    ones = jnp.full((HEAD_SIZE, HEAD_SIZE), 1.0 / HEAD_SIZE, BF16)
    return nn(values.astype(BF16), ones)


def rope_tables():
    position = jnp.arange(SEQ_LEN).astype(F32)
    inverse = jnp.power(rope_base, -jnp.arange(HEAD_SIZE // 2).astype(F32) * (2.0 / HEAD_SIZE))
    angles = position[:, None] * inverse[None, :]
    cosine, sine = jnp.cos(angles), jnp.sin(angles)
    return (
        jnp.concatenate([cosine, cosine], axis=1),
        jnp.concatenate([-sine, sine], axis=1),
    )


def params(*semantics):
    return pltpu.CompilerParams(dimension_semantics=semantics, vmem_limit_bytes=VMEM_LIMIT)


def cost(flops, rate):
    return pl.CostEstimate(flops=int(flops * (1000.0 / rate)), bytes_accessed=0, transcendentals=0)


def whole(shape):
    return pl.BlockSpec(shape, lambda *_: (0,) * len(shape), pipeline_mode=pl.Buffered(1))


def out_weight_spec(width, heads):
    return pl.BlockSpec((width, heads), lambda *_: (0, 2), pipeline_mode=pl.Buffered(1))


def project_kernel(x_ref, gain_ref, w_ref, qn_ref, kn_ref, cos_ref, sin_ref, at_ref, raw_ref, rot_ref):
    x = x_ref[...].astype(F32)
    scale = lax.rsqrt(jnp.mean(x * x, axis=-1, keepdims=True) + epsilon)
    a = (x * scale * gain_ref[...]).astype(BF16)
    at_ref[...] = a.T
    cosine, sine = cos_ref[...], sin_ref[...]
    for group in range(w_ref.shape[1] // GROUP):
        base = group * GROUP
        y = nn(a, w_ref[:, base : base + GROUP])
        raw_ref[:, base : base + GROUP] = y.astype(BF16)
        for head in range(3):
            z = y[:, head * HEAD_SIZE : (head + 1) * HEAD_SIZE]
            gain = kn_ref[...] * (SCORE_SCALE / LN2) if head == 2 else qn_ref[...]
            z = z * lax.rsqrt(jnp.mean(z * z, axis=-1, keepdims=True) + epsilon) * gain
            z = z * cosine + pltpu.roll(z, HEAD_SIZE // 2, 1) * sine
            rot_ref[:, base + head * HEAD_SIZE : base + (head + 1) * HEAD_SIZE] = z.astype(BF16)
        rot_ref[:, base + 3 * HEAD_SIZE : base + GROUP] = y[:, 3 * HEAD_SIZE :].astype(BF16)


def project(x, gain, weights, query_norm, key_norm, cosine, sine):
    tokens, width = x.shape
    columns = weights.shape[1] // 3 * 2
    rows = 256
    return pl.pallas_call(
        project_kernel,
        grid=(tokens // rows,),
        in_specs=[
            pl.BlockSpec((rows, width), lambda i: (i, 0)),
            whole((1, width)),
            whole((width, columns)),
            whole((1, HEAD_SIZE)),
            whole((1, HEAD_SIZE)),
            pl.BlockSpec((rows, HEAD_SIZE), lambda i: (i, 0)),
            pl.BlockSpec((rows, HEAD_SIZE), lambda i: (i, 0)),
        ],
        out_specs=[
            pl.BlockSpec((width, rows), lambda i: (0, i)),
            pl.BlockSpec((rows, columns), lambda i: (i, 0)),
            pl.BlockSpec((rows, columns), lambda i: (i, 0)),
        ],
        out_shape=[
            jax.ShapeDtypeStruct((width, tokens), BF16),
            jax.ShapeDtypeStruct((tokens, columns), BF16),
            jax.ShapeDtypeStruct((tokens, columns), BF16),
        ],
        compiler_params=params("arbitrary"),
        cost_estimate=cost(2 * tokens * width * columns, 500),
        name="project",
    )(x, gain, weights, query_norm, key_norm, cosine, sine)


BLOCK = 512


def split_three(values):
    lane = lax.broadcasted_iota(jnp.int32, values.shape, 1)
    high = values.astype(BF16).astype(F32)
    rest = values - high
    middle = rest.astype(BF16).astype(F32)
    low = rest - middle
    return jnp.where(
        lane == 0, high, jnp.where(lane == 1, middle, jnp.where(lane == 2, low, 0.0))
    ).astype(BF16)


def attend_kernel(first, q_ref, k_ref, v_ref, out_ref, log_ref, v_ones, acc):
    i = pl.program_id(1)

    @pl.when(i == 0)
    def _():
        v_ones[:, :HEAD_SIZE] = v_ref[...]
        v_ones[:, HEAD_SIZE:] = jnp.ones(v_ref.shape, BF16)

    acc[...] = jnp.zeros_like(acc)

    def tile(row, rows, start, size, masked):
        keys = k_ref[pl.ds(start, size), :]
        values = v_ones[pl.ds(start, size), :]
        for head in range(2):
            s = nt(q_ref[row : row + rows, head * HEAD_SIZE : (head + 1) * HEAD_SIZE], keys)
            if masked:
                query = lax.broadcasted_iota(jnp.int32, s.shape, 0)
                key = lax.broadcasted_iota(jnp.int32, s.shape, 1)
                s = jnp.where(key <= query + (size - rows), s, masked_score)
            acc[head, row : row + rows] += nn(jnp.exp2(s).astype(BF16), values)

    def step(j, carry):
        tile(0, BLOCK, pl.multiple_of(j * BLOCK, BLOCK), BLOCK, False)
        return carry

    lax.fori_loop(0, i + first, step, 0)
    start = pl.multiple_of((i + first) * BLOCK, BLOCK)
    tile(0, BLOCK // 2, start, BLOCK // 2, True)
    tile(BLOCK // 2, BLOCK // 2, start, BLOCK, True)
    for head in range(2):
        columns = slice(head * HEAD_SIZE, (head + 1) * HEAD_SIZE)
        total = acc[head, :, HEAD_SIZE:]
        out_ref[:, columns] = (acc[head, :, :HEAD_SIZE] / total).astype(BF16)
        log_ref[:, columns] = split_three(jnp.log(total) * (-1.0 / LN2))


def attend(rot, half):
    groups = rot.shape[1] // GROUP
    width = 2 * HEAD_SIZE
    blocks = HALF // BLOCK
    first = half * blocks
    keys = HALF * (half + 1)
    return pl.pallas_call(
        lambda *refs: attend_kernel(first, *refs),
        grid=(groups, blocks),
        in_specs=[
            pl.BlockSpec((BLOCK, width), lambda c, i: (i + first, 2 * c)),
            pl.BlockSpec((keys, HEAD_SIZE), lambda c, i: (0, 4 * c + 2)),
            pl.BlockSpec((keys, HEAD_SIZE), lambda c, i: (0, 4 * c + 3)),
        ],
        out_specs=[
            pl.BlockSpec((BLOCK, width), lambda c, i: (i, c)),
            pl.BlockSpec((BLOCK, width), lambda c, i: (i, c)),
        ],
        out_shape=[
            jax.ShapeDtypeStruct((HALF, groups * width), BF16),
            jax.ShapeDtypeStruct((HALF, groups * width), BF16),
        ],
        scratch_shapes=[
            pltpu.VMEM((keys, width), BF16),
            pltpu.VMEM((2, BLOCK, width), F32),
        ],
        compiler_params=params("arbitrary", "arbitrary"),
        cost_estimate=cost(4 * HALF * keys * groups * width, 500),
        name="attend",
    )(rot, rot, rot)


def out_project_kernel(mixed_ref, w_ref, out_ref):
    out_ref[...] = nt(mixed_ref[...], w_ref[...]).astype(BF16)


def out_project(mixed, weights):
    rows = 256
    width, heads = weights.shape[0], mixed.shape[1]
    return pl.pallas_call(
        out_project_kernel,
        grid=(HALF // rows,),
        in_specs=[
            pl.BlockSpec((rows, heads), lambda i: (i, 0)),
            out_weight_spec(width, heads),
        ],
        out_specs=pl.BlockSpec((rows, width), lambda i: (i, 0)),
        out_shape=jax.ShapeDtypeStruct((HALF, width), BF16),
        compiler_params=params("arbitrary"),
        cost_estimate=cost(2 * HALF * width * heads, 350),
        name="out_project",
    )(mixed, weights)


ROWS = 256


def attend_back_kernel(
    rot_ref, raw_ref, do_a, do_b, out_a, out_b, log_a, log_b, qn_ref, kn_ref, cos_ref, sin_ref,
    bits_ref, qg_ref, kg_ref,
    grads, log_row, delta_row, k_flip, dq_flip, dk, dv,
):
    blocks = SEQ_LEN // BLOCK
    ones = jnp.ones((8, HEAD_SIZE), BF16)

    def prepare(half, do_ref, out_ref, log_ref):
        def body(r, carry):
            near = pl.ds(pl.multiple_of(r * ROWS, ROWS), ROWS)
            rows = pl.ds(pl.multiple_of(half * HALF + r * ROWS, ROWS), ROWS)
            k_flip[:, rows] = rot_ref[rows, 2 * HEAD_SIZE : 3 * HEAD_SIZE].T
            grad = do_ref[near, :]
            grads[rows, :] = grad
            product = grad.astype(F32) * out_ref[near, :].astype(F32)
            high = product.astype(BF16)
            low = (product - high.astype(F32)).astype(BF16)
            for head in range(2):
                columns = slice(head * HEAD_SIZE, (head + 1) * HEAD_SIZE)
                log_row[head, :, rows] = nt(ones, log_ref[near, columns])
                delta_row[head, :, rows] = nt(ones, high[:, columns]) + nt(ones, low[:, columns])
            return carry

        lax.fori_loop(0, HALF // ROWS, body, 0)

    prepare(0, do_a, out_a, log_a)
    prepare(1, do_b, out_b, log_b)
    dq_flip[...] = jnp.zeros_like(dq_flip)

    def tile(kv_start, kv_size, start, size, masked):
        kv, q_rows = pl.ds(kv_start, kv_size), pl.ds(start, size)
        keys = rot_ref[kv, 2 * HEAD_SIZE : 3 * HEAD_SIZE]
        values = rot_ref[kv, 3 * HEAD_SIZE :]
        for head in range(2):
            columns = slice(head * HEAD_SIZE, (head + 1) * HEAD_SIZE)
            q = rot_ref[q_rows, columns]
            d = grads[q_rows, columns]
            s = nt(keys, q) + log_row[head, :1, q_rows]
            if masked:
                row = lax.broadcasted_iota(jnp.int32, s.shape, 0)
                column = lax.broadcasted_iota(jnp.int32, s.shape, 1)
                s = jnp.where(row <= column, s, masked_score)
            p = jnp.exp2(s)
            ds = (p * (nt(values, d) - delta_row[head, :1, q_rows])).astype(BF16)
            new_dv = nn(p.astype(BF16), d)
            new_dk = nn(ds, q)
            if masked and head == 0:
                dv[kv, :] = new_dv
                dk[kv, :] = new_dk
            else:
                dv[kv, :] += new_dv
                dk[kv, :] += new_dk
            dq_flip[head, :, q_rows] += nn(k_flip[:, kv], ds)

    part = BLOCK // 2

    def key_block(j, carry):
        start = pl.multiple_of(j * BLOCK, BLOCK)
        later = pl.multiple_of(j * BLOCK + part, part)
        tile(start, part, start, BLOCK, True)
        tile(later, part, later, part, True)

        def query_block(i, inner):
            tile(start, BLOCK, pl.multiple_of(i * BLOCK, BLOCK), BLOCK, False)
            return inner

        return lax.fori_loop(j + 1, blocks, query_block, carry)

    lax.fori_loop(0, blocks, key_block, 0)

    qg_ref[...] = jnp.zeros_like(qg_ref)
    kg_ref[...] = jnp.zeros_like(kg_ref)

    def finish(r, carry):
        rows = pl.ds(pl.multiple_of(r * ROWS, ROWS), ROWS)
        cosine, sine = cos_ref[rows, :], sin_ref[rows, :]
        for head in range(3):
            columns = slice(head * HEAD_SIZE, (head + 1) * HEAD_SIZE)
            if head < 2:
                u = dq_flip[head, :, rows].T * LN2
                gain, total = qn_ref[...], qg_ref
            else:
                u = dk[rows, :] * SCORE_SCALE
                gain, total = kn_ref[...], kg_ref
            u = u * cosine - pltpu.roll(u, HEAD_SIZE // 2, 1) * sine
            x = raw_ref[rows, columns].astype(F32)
            scale = lax.rsqrt(row_mean(x * x) + epsilon)
            x = x * scale
            total[0] += jnp.sum((u * x).reshape(ROWS // 8, 8, HEAD_SIZE), axis=0)
            w = u * gain
            bits_ref[rows, columns] = (
                scale * (w - x * row_mean(w * x))
            ).astype(BF16)
        bits_ref[rows, 3 * HEAD_SIZE :] = dv[rows, :].astype(BF16)
        return carry

    lax.fori_loop(0, SEQ_LEN // ROWS, finish, 0)


def attend_back(rot, raw, grads, outs, logs, query_norm, key_norm, cosine, sine):
    groups = rot.shape[1] // GROUP
    width = 2 * HEAD_SIZE
    return pl.pallas_call(
        attend_back_kernel,
        grid=(groups,),
        in_specs=[
            pl.BlockSpec((SEQ_LEN, GROUP), lambda c: (0, c)),
            pl.BlockSpec((SEQ_LEN, GROUP), lambda c: (0, c)),
            *[pl.BlockSpec((HALF, width), lambda c: (0, c))] * 6,
            whole((1, HEAD_SIZE)),
            whole((1, HEAD_SIZE)),
            whole((SEQ_LEN, HEAD_SIZE)),
            whole((SEQ_LEN, HEAD_SIZE)),
        ],
        out_specs=[
            pl.BlockSpec((SEQ_LEN, GROUP), lambda c: (0, c)),
            pl.BlockSpec((1, 8, HEAD_SIZE), lambda c: (c, 0, 0)),
            pl.BlockSpec((1, 8, HEAD_SIZE), lambda c: (c, 0, 0)),
        ],
        out_shape=[
            jax.ShapeDtypeStruct((SEQ_LEN, groups * GROUP), BF16),
            jax.ShapeDtypeStruct((groups, 8, HEAD_SIZE), F32),
            jax.ShapeDtypeStruct((groups, 8, HEAD_SIZE), F32),
        ],
        scratch_shapes=[
            pltpu.VMEM((SEQ_LEN, width), BF16),
            pltpu.VMEM((2, 8, SEQ_LEN), F32),
            pltpu.VMEM((2, 8, SEQ_LEN), F32),
            pltpu.VMEM((HEAD_SIZE, SEQ_LEN), BF16),
            pltpu.VMEM((2, HEAD_SIZE, SEQ_LEN), F32),
            pltpu.VMEM((SEQ_LEN, HEAD_SIZE), F32),
            pltpu.VMEM((SEQ_LEN, HEAD_SIZE), F32),
        ],
        compiler_params=params("arbitrary"),
        cost_estimate=cost(5 * SEQ_LEN * SEQ_LEN * groups * width, 80),
        name="attend_back",
    )(rot, raw, *grads, *outs, *logs, query_norm, key_norm, cosine, sine)


def residual_of(x_ref, own_ref, other_ref):
    residual = x_ref[...].astype(F32) + (own_ref[...].astype(F32) + other_ref[...].astype(F32))
    scale = lax.rsqrt(jnp.mean(residual * residual, axis=-1, keepdims=True) + epsilon)
    return residual * scale, scale


def middle_kernel(
    x_ref, own_ref, other_ref, grad_ref, fn_ref, w_ref, down_ref, flip_ref, y_ref, fg_ref
):
    width, columns = w_ref.shape
    hidden = columns // 3
    chunk = 512 if hidden % 512 == 0 else hidden
    rows = x_ref.shape[0]
    normed, scale = residual_of(x_ref, own_ref, other_ref)
    f = (normed * fn_ref[...]).astype(BF16)
    grad = grad_ref[...]
    flip_ref[0] = f.T
    flip_ref[1] = grad.T
    total = jnp.zeros((rows, width), F32)
    f_grad = jnp.zeros((rows, width), F32)
    for start in range(0, hidden, chunk):
        gate_w = w_ref[:, start : start + chunk]
        up_w = w_ref[:, hidden + start : hidden + start + chunk]
        down_w = w_ref[:, 2 * hidden + start : 2 * hidden + start + chunk]
        gate, up = nn(f, gate_w), nn(f, up_w)
        sig = 1.0 / (1.0 + jnp.exp(-gate))
        silu = gate * sig
        low = (silu * up).astype(BF16)
        total += nt(low, down_w)
        hidden_grad = nn(grad, down_w)
        gate_bits = (hidden_grad * up * (sig * (1.0 + gate * (1.0 - sig)))).astype(BF16)
        up_bits = (hidden_grad * silu).astype(BF16)
        y_ref[:, start : start + chunk] = gate_bits
        y_ref[:, hidden + start : hidden + start + chunk] = up_bits
        y_ref[:, 2 * hidden + start : 2 * hidden + start + chunk] = low
        f_grad += nt(gate_bits, gate_w) + nt(up_bits, up_w)
    down_ref[...] = total.astype(BF16)
    fg_ref[...] = f_grad.astype(BF16)


def half_rows(rows, width, half):
    return pl.BlockSpec((rows, width), lambda i: (i + half * (HALF // rows), 0))


def middle(half, x_all, own, other, grad_all, gain, weights):
    width, columns = weights.shape
    rows = 512
    near = pl.BlockSpec((rows, width), lambda i: (i, 0))
    return pl.pallas_call(
        middle_kernel,
        grid=(HALF // rows,),
        in_specs=[
            half_rows(rows, width, half), near, near, half_rows(rows, width, half),
            whole((1, width)), whole(weights.shape),
        ],
        out_specs=[
            near,
            pl.BlockSpec((2, width, rows), lambda i: (0, 0, i)),
            pl.BlockSpec((rows, columns), lambda i: (i, 0)),
            near,
        ],
        out_shape=[
            jax.ShapeDtypeStruct((HALF, width), BF16),
            jax.ShapeDtypeStruct((2, width, HALF), BF16),
            jax.ShapeDtypeStruct((HALF, columns), BF16),
            jax.ShapeDtypeStruct((HALF, width), BF16),
        ],
        compiler_params=params("arbitrary"),
        cost_estimate=cost(4 * HALF * width * columns, 2500),
        name="middle",
    )(x_all, own, other, grad_all, gain, weights)


def residual_back_kernel(
    x_ref, own_ref, other_ref, grad_ref, fg_ref, fg_other_ref, fn_ref, w_ref,
    rg_ref, flip_ref, mg_ref, fng_ref,
):
    rows, width = x_ref.shape
    normed, scale = residual_of(x_ref, own_ref, other_ref)
    f_grad = fg_ref[...].astype(F32) + fg_other_ref[...].astype(F32)

    @pl.when(pl.program_id(0) == 0)
    def _():
        fng_ref[...] = jnp.zeros_like(fng_ref)

    fng_ref[...] += jnp.sum((f_grad * normed).reshape(rows // 8, 8, width), axis=0)
    u = f_grad * fn_ref[...]
    residual_grad = grad_ref[...].astype(F32) + scale * (
        u - normed * jnp.mean(u * normed, axis=-1, keepdims=True)
    )
    rg_ref[...] = residual_grad
    proj = residual_grad.astype(BF16)
    flip_ref[...] = proj.T
    mg_ref[...] = nn(proj, w_ref[...]).astype(BF16)


def residual_back(half, x_all, own, other, grad_all, fg, fg_other, gain, weights, heads):
    width = weights.shape[0]
    rows = 256
    near = pl.BlockSpec((rows, width), lambda i: (i, 0))
    return pl.pallas_call(
        residual_back_kernel,
        grid=(HALF // rows,),
        in_specs=[
            half_rows(rows, width, half), near, near, half_rows(rows, width, half), near, near,
            whole((1, width)), out_weight_spec(width, heads),
        ],
        out_specs=[
            near,
            pl.BlockSpec((width, rows), lambda i: (0, i)),
            pl.BlockSpec((rows, heads), lambda i: (i, 0)),
            pl.BlockSpec((8, width), lambda i: (0, 0)),
        ],
        out_shape=[
            jax.ShapeDtypeStruct((HALF, width), F32),
            jax.ShapeDtypeStruct((width, HALF), BF16),
            jax.ShapeDtypeStruct((HALF, heads), BF16),
            jax.ShapeDtypeStruct((8, width), F32),
        ],
        compiler_params=params("arbitrary"),
        cost_estimate=cost(2 * HALF * width * heads, 190),
        name="residual_back",
    )(x_all, own, other, grad_all, fg, fg_other, gain, weights)


def middle_weights_kernel(which, flip_a, flip_b, y_a, y_b, *rest):
    rest[-1][...] = (nn(flip_a[which], y_a[...]) + nn(flip_b[which], y_b[...])).astype(BF16)


def middle_weights(flips, ys, down, *partial):
    width = flips[0].shape[1]
    columns = ys[0].shape[1]
    hidden = columns // 3
    size = 512 if hidden % 512 == 0 else hidden
    bound = 2 * hidden // size
    first, blocks = (bound, columns // size - bound) if down else (0, bound)
    which = 1 if down else 0
    spec = pl.BlockSpec((HALF, size), lambda i: (0, i + first))
    flip_spec = pl.BlockSpec(
        (1, width, HALF), lambda i: (which, 0, 0), pipeline_mode=pl.Buffered(1)
    )
    return pl.pallas_call(
        lambda *refs: middle_weights_kernel(0, *refs),
        grid=(blocks,),
        in_specs=[flip_spec, flip_spec, spec, spec] + [pl.BlockSpec(memory_space=pl.ANY)] * len(partial),
        out_specs=pl.BlockSpec((width, size), lambda i: (0, i + first)),
        out_shape=jax.ShapeDtypeStruct((width, columns), BF16),
        input_output_aliases={4: 0} if partial else {},
        compiler_params=params("arbitrary"),
        cost_estimate=cost(2 * SEQ_LEN * width * size * blocks, 3000),
        name="down_weights" if down else "gate_up_weights",
    )(*flips, *ys, *partial)


def attention_weights_kernel(
    bound, input_flip, proj_a, proj_b, bits_ref, mixed_a, mixed_b, w_ref, out_ref, sums_ref
):
    i = pl.program_id(0)

    @pl.when(i == 0)
    def _():
        sums_ref[...] = jnp.zeros_like(sums_ref)

    @pl.when(i < bound)
    def _():
        out = nn(input_flip[...], bits_ref[...])
        out_ref[...] = out.astype(BF16)
        product = out * w_ref[...].astype(F32)
        for start in range(0, product.shape[1], 128):
            sums_ref[...] += product[:, start : start + 128]

    @pl.when(i >= bound)
    def _():
        out_ref[...] = (nn(proj_a[...], mixed_a[...]) + nn(proj_b[...], mixed_b[...])).astype(BF16)


def attention_weights(input_flip, projs, bits, mixed, weights):
    width, columns = weights.shape
    heads = columns // 3
    size = math.gcd(512, heads)
    bound = 2 * heads // size
    mixed_spec = pl.BlockSpec((HALF, size), lambda i: (0, jnp.maximum(i - bound, 0)))
    return pl.pallas_call(
        lambda *refs: attention_weights_kernel(bound, *refs),
        grid=(columns // size,),
        in_specs=[
            whole(input_flip.shape), whole(projs[0].shape), whole(projs[1].shape),
            pl.BlockSpec((SEQ_LEN, size), lambda i: (0, jnp.minimum(i, bound - 1))),
            mixed_spec, mixed_spec,
            pl.BlockSpec((width, size), lambda i: (0, i)),
        ],
        out_specs=[
            pl.BlockSpec((width, size), lambda i: (0, i)),
            pl.BlockSpec((width, 128), lambda i: (0, 0)),
        ],
        out_shape=[
            jax.ShapeDtypeStruct((width, columns), BF16),
            jax.ShapeDtypeStruct((width, 128), F32),
        ],
        compiler_params=params("arbitrary"),
        cost_estimate=cost(2 * SEQ_LEN * width * columns, 640),
        name="attention_weights",
    )(input_flip, *projs, bits, *mixed, weights)


def input_back_kernel(place_ref, bits_ref, w_ref, out_ref):
    out_ref[...] = nt(bits_ref[...], w_ref[...]).astype(BF16)


def input_back(place, tokens, bits, weights):
    width = weights.shape[0]
    columns = bits.shape[1]
    rows = 256
    blocks = tokens // rows
    return pl.pallas_call(
        input_back_kernel,
        grid_spec=pltpu.PrefetchScalarGridSpec(
            num_scalar_prefetch=1,
            grid=(blocks,),
            in_specs=[
                pl.BlockSpec((rows, columns), lambda i, place: (place[0] * blocks + i, 0)),
                whole((width, columns)),
            ],
            out_specs=pl.BlockSpec((rows, width), lambda i, place: (i, 0)),
        ),
        out_shape=jax.ShapeDtypeStruct((tokens, width), BF16),
        compiler_params=params("arbitrary"),
        cost_estimate=cost(2 * tokens * width * columns, 480),
        name="input_back",
    )(place.reshape(1), bits, weights)


def swap(values):
    return lax.ppermute(values, "tensor", [(0, 1), (1, 0)])


def in_order(own, other, axis):
    first = lax.axis_index("tensor") == 0
    return jnp.concatenate(
        [jnp.where(first, own, other), jnp.where(first, other, own)], axis=axis
    )


def send_tokens(values, ranks):
    if ranks == 2:
        return swap(values)
    return lax.all_gather(values, "tensor", axis=0, tiled=True)


def all_tokens(own, sent, ranks):
    return in_order(own, sent, 0) if ranks == 2 else sent


def others_sum(values, ranks):
    if ranks == 2:
        return swap(values)
    own = values.astype(F32)
    return (lax.psum(own, "tensor") - own).astype(BF16)


def own_rows(halves, ranks, me, rows):
    if ranks == 2:
        return jnp.where(me == 0, halves[0], halves[1])
    return lax.dynamic_slice_in_dim(jnp.concatenate(halves, axis=0), me * rows, rows)


def sum_over_all(values, devices):
    if devices & (devices - 1):
        return lax.psum(values, ("dp", "tensor"))
    step = 1
    while step < devices:
        pairs = [(device, device ^ step) for device in range(devices)]
        values = values + lax.ppermute(values, ("dp", "tensor"), pairs)
        step *= 2
    return values


def after(values, *events):
    return lax.optimization_barrier((values, *events))[0]


def on_device(
    layer_input,
    attention_norm,
    query_weight,
    key_matrix,
    value_matrix,
    query_norm,
    key_norm,
    output_weight,
    feedforward_norm,
    gate_weight,
    up_weight,
    down_weight,
    out_grad,
):
    ranks = lax.axis_size("tensor")
    me = lax.axis_index("tensor")
    depth = query_weight.shape[0]
    tok_rows, width = layer_input.shape
    groups = key_matrix.shape[1] // HEAD_SIZE
    heads = query_weight.shape[1]
    hidden = gate_weight.shape[1]

    own_attention = jnp.concatenate(
        [
            jnp.concatenate(
                [
                    query_weight.reshape(depth, groups, 2 * HEAD_SIZE),
                    key_matrix.reshape(depth, groups, HEAD_SIZE),
                    value_matrix.reshape(depth, groups, HEAD_SIZE),
                ],
                axis=2,
            ).reshape(depth, groups * GROUP),
            output_weight.T,
        ],
        axis=1,
    )
    attention_w = lax.all_gather(own_attention, "dp", axis=0, tiled=True)
    x_sent = send_tokens(layer_input, ranks)
    x_all = all_tokens(layer_input, x_sent, ranks)
    own_middle = jnp.concatenate([gate_weight, up_weight, down_weight.T], axis=1)
    middle_w = lax.all_gather(own_middle, "dp", axis=0, tiled=True)
    grad_sent = send_tokens(after(out_grad, x_sent), ranks)

    cosine, sine = rope_tables()
    norm_q, norm_k = query_norm[None, :], key_norm[None, :]
    norm_two = feedforward_norm[None, :]
    input_flip, raw, rot = project(
        x_all, attention_norm[None, :], attention_w, norm_q, norm_k, cosine, sine
    )
    mixed, logs, owns, others = [], [], [], []
    for half in range(2):
        out, log = attend(after(rot, *owns), half)
        mixed.append(out)
        logs.append(log)
        owns.append(out_project(out, attention_w))
        others.append(others_sum(after(owns[half], *others), ranks))

    grad_all = all_tokens(after(out_grad, owns[0]), grad_sent, ranks)

    downs, flips, ys, f_grads, f_others = [], [], [], [], []
    for half in range(2):
        down, flip, y, f_grad = middle(
            half, after(x_all, *downs), owns[half], others[half], grad_all, norm_two, middle_w
        )
        downs.append(down)
        flips.append(flip)
        ys.append(y)
        f_grads.append(f_grad)
        if half == 0:
            f_others.append(others_sum(f_grad, ranks))
    down_part = middle_weights(flips, ys, True)
    f_others.append(others_sum(after(f_grads[1], f_others[0], down_part), ranks))
    middle_part = middle_weights(flips, ys, False, down_part)
    middle_sum = lax.psum_scatter(middle_part, "dp", scatter_dimension=0, tiled=True)
    middle_grad = middle_sum.astype(F32)

    f_others[1] = after(f_others[1], middle_part)

    residual_grads, projs, mixed_grads, norm_two_part = [], [], [], 0.0
    for half in range(2):
        residual_grad, proj, mixed_grad, part = residual_back(
            half, after(x_all, *projs), owns[half], others[half], grad_all, f_grads[half], f_others[half],
            norm_two, attention_w, heads,
        )
        residual_grads.append(residual_grad)
        projs.append(proj)
        mixed_grads.append(mixed_grad)
        norm_two_part = norm_two_part + jnp.sum(part, axis=0) / ranks

    bits, query_part, key_part = attend_back(
        rot, raw, mixed_grads, mixed, logs, norm_q, norm_k, cosine, sine
    )

    if ranks == 2:
        send = after(jnp.where(me == 0, downs[1], downs[0]), mixed_grads[1])
        down_other = swap(send)
        bits = after(bits, down_other)
        down_sum = own_rows(downs, ranks, me, tok_rows).astype(F32) + down_other.astype(F32)
    else:
        down_sum = lax.psum_scatter(
            jnp.concatenate(downs, axis=0).astype(F32), "tensor", scatter_dimension=0, tiled=True
        )
    x = layer_input.astype(F32)
    residual = x + (
        own_rows(owns, ranks, me, tok_rows).astype(F32)
        + own_rows(others, ranks, me, tok_rows).astype(F32)
    )
    layer_output = (residual + down_sum).astype(BF16)

    bits = after(bits, middle_sum)
    attention_part, sums = attention_weights(input_flip, projs, bits, mixed, attention_w)
    attention_grad = lax.psum_scatter(
        attention_part, "dp", scatter_dimension=0, tiled=True
    ).astype(F32)
    norm_one_part = jnp.sum(sums, axis=1) / attention_norm
    if ranks == 2:
        other = swap(input_back(1 - me, tok_rows, bits, attention_w))
        own = input_back(me, tok_rows, bits, attention_w)
        attention_input_grad = own.astype(F32) + other.astype(F32)
    else:
        attention_input_grad = lax.psum_scatter(
            input_back(jnp.zeros_like(me), SEQ_LEN, bits, attention_w).astype(F32),
            "tensor",
            scatter_dimension=0,
            tiled=True,
        )
    scale = lax.rsqrt(jnp.mean(x * x, axis=-1, keepdims=True) + epsilon)
    normed = x * scale
    u = attention_input_grad * attention_norm
    input_grad = own_rows(residual_grads, ranks, me, tok_rows) + scale * (
        u - normed * jnp.mean(u * normed, axis=-1, keepdims=True)
    )
    sums = sum_over_all(
        jnp.concatenate(
            [
                norm_one_part,
                norm_two_part,
                jnp.sum(query_part, axis=(0, 1)),
                jnp.sum(key_part, axis=(0, 1)),
            ]
        ).reshape(-1, HEAD_SIZE),
        lax.axis_size("dp") * ranks,
    ).reshape(-1)
    attention_norm_grad, feedforward_norm_grad, query_norm_grad, key_norm_grad = jnp.split(
        sums, [width, 2 * width, 2 * width + HEAD_SIZE]
    )
    qkv_grad = attention_grad[:, : groups * GROUP].reshape(depth, groups, GROUP)
    return (
        layer_output,
        input_grad,
        attention_norm_grad,
        qkv_grad[:, :, : 2 * HEAD_SIZE].reshape(depth, -1),
        qkv_grad[:, :, 2 * HEAD_SIZE : 3 * HEAD_SIZE].reshape(depth, -1),
        qkv_grad[:, :, 3 * HEAD_SIZE :].reshape(depth, -1),
        query_norm_grad,
        key_norm_grad,
        attention_grad[:, groups * GROUP :].T,
        feedforward_norm_grad,
        middle_grad[:, :hidden],
        middle_grad[:, hidden : 2 * hidden],
        middle_grad[:, 2 * hidden :].T,
    )


def solution(mesh):
    return jax.shard_map(
        on_device,
        mesh=mesh,
        in_specs=(
            P(("dp", "tensor"), None),
            P(),
            P("dp", "tensor"),
            P("dp", "tensor"),
            P("dp", "tensor"),
            P(),
            P(),
            P("tensor", "dp"),
            P(),
            P("dp", "tensor"),
            P("dp", "tensor"),
            P("tensor", "dp"),
            P(("dp", "tensor"), None),
        ),
        out_specs=(
            P(("dp", "tensor"), None),
            P(("dp", "tensor"), None),
            P(),
            P("dp", "tensor"),
            P("dp", "tensor"),
            P("dp", "tensor"),
            P(),
            P(),
            P("tensor", "dp"),
            P(),
            P("dp", "tensor"),
            P("dp", "tensor"),
            P("tensor", "dp"),
        ),
        check_vma=False,
    )
```
